128 devices in a mesh: gx: 8 (over z, core), yz: 16 (over y, x).
Axes of the slice: x: 4, y: 4, z: 4, core: 2. Of those that a mesh axis runs over, the one named last changes fastest.
Arguments:
- field: float32 [144, 262144], P(None, ('gx', 'yz')), may hold values from -6 to 6
- edge_signs: int32 [12, 262144], P(None, ('gx', 'yz')), may hold values from -1 to 1, as said below
- face_nbrs: int32 [6, 262144], P(None, ('gx', 'yz')), may hold values from -1 to 262143, as said below
- elem_size: float32 [262144], P(('gx', 'yz')), may hold values from 0.5 to 2
- mu_inv: float32 [262144], P(('gx', 'yz')), may hold values from 0.25 to 4
- permittivity: float32 [262144], P(('gx', 'yz')), may hold values from 0.25 to 4
- new_owner: int32 [262144, 1], P(('gx', 'yz')), may hold values from 0 to 127; in each aligned block of 2048 rows (0 to 2047, 2048 to 4095, ...) at most 32 rows name the same one
- trace_map: float32 [144, 144], replicated, may hold values from -0.5 to 0.5
- stiffness: float32 [144, 144], replicated, may hold values from -0.5 to 0.5
- mass: float32 [144, 144], replicated, may hold values from -0.5 to 0.5
Outputs:
- indicators: float32 [262144], P(('gx', 'yz'))
- migrated: float32 [144, 524288], P(None, ('gx', 'yz'))
- applied: float32 [144, 524288], P(None, ('gx', 'yz'))
The draws below stay inside these ranges and needn't reach their ends.
Inputs may be any that keep to these rules, and one draw needn't show every extreme that they name: `edge_signs`: each entry is -1 or 1. `face_nbrs`: A neighbour of an element of device block b (elements b * 2048 to (b + 1) * 2048 - 1) lies in block b - 1, b or b + 1, or is -1. `new_owner`: within the elements of one device no device number appears more than 32 times, and some device receives exactly 32 from some device.
All inputs are finite; a program needn't handle non-finite values.
Results may differ from the reference program's by a relative error of at most 0.0003.
Values sent between devices are 32-bit elements; how exact they have to be, the bound alone decides.
A program may use at most 64 MiB of HBM per device.

```python
import math
import jax
import jax.numpy as jnp
import numpy as np
from jax import lax

DOFS = 144
FT = 24
E_DEV = 2048
ELEMS = 262144
CAP = 32
SLOTS = 524288
N_GX = 8
N_YZ = 16


def draw_edge_signs(key, part):
    bits = jax.random.randint(jax.random.fold_in(key, 7), (12, ELEMS), 0, 2)
    return (2 * bits - 1).astype(jnp.int32)


def draw_face_nbrs(key, part):
    keys = jax.random.split(jax.random.fold_in(key, 11), 3)
    nblocks = ELEMS // E_DEV
    block = jnp.arange(ELEMS, dtype=jnp.int32) // E_DEV
    side = jax.random.randint(keys[0], (6, ELEMS), -1, 2)
    target = jnp.clip(block[None, :] + side, 0, nblocks - 1)
    local = jax.random.randint(keys[1], (6, ELEMS), 0, E_DEV)
    nbr = target * E_DEV + local
    edge = jax.random.randint(keys[2], (6, ELEMS), 0, 8) == 0
    nbr = jnp.where(edge, -1, nbr)
    nbr = nbr.at[0, 0].set(-1).at[0, ELEMS - 1].set(ELEMS - 1)
    return nbr.astype(jnp.int32)


def block_levels(key, extent, shards, least, largest):
    def one(position, parts):
        draws = jax.random.uniform(jax.random.fold_in(jax.random.fold_in(key, 6), position), (parts,), jnp.float32, least / len(shards), largest / len(shards))
        return jnp.repeat(jnp.exp(draws), extent[position] // parts).reshape((-1,) + (1,) * (len(extent) - position - 1))

    loudness = one(*shards[0])
    for cut in shards[1:]:
        loudness = loudness * one(*cut)
    return loudness


def shared_out(rng, own, number, rows, amount, top, most, lean):
    order = jax.random.permutation(rng, amount)
    heavy_load, usual = portions_of(amount, rows * top, most, lean, True), portions_of(amount, rows * top, most, lean, False)
    places = jnp.arange(amount)

    def named(tallies, offset_by):
        used = int((tallies > 0).sum())
        fixed = max(1, used // 4)
        moved = fixed + (places - fixed + offset_by * (used - fixed)) % max(1, amount - fixed)
        return jnp.zeros((amount,), jnp.int32).at[order[jnp.where(places < fixed, places, moved)]].set(jnp.asarray(tallies, jnp.int32))

    tallies = jnp.where(number % 4 == 0, named(heavy_load, number // 4), named(usual, number - number // 4 - 1))
    mixed = jax.random.permutation(jax.random.fold_in(own, 3), amount)
    source_of, sink = mixed[0:amount // 2 * 2:2], mixed[1:amount // 2 * 2:2]
    room = jnp.minimum(tallies[source_of] - 1, most - tallies[sink]) // 2
    room = jnp.where((source_of == order[0]) | (sink == order[0]) | (tallies[sink] == 0), 0, jnp.maximum(room, 0))
    moved = jax.random.randint(jax.random.fold_in(own, 4), (amount // 2,), 0, 1 << 20) % (room + 1)
    tallies = tallies.at[source_of].add(-moved).at[sink].add(moved)
    labels = jnp.searchsorted(jnp.cumsum(tallies), jnp.arange(rows * top), side="right").astype(jnp.int32)
    table = labels.reshape(top, rows).T
    table = table[jax.random.permutation(jax.random.fold_in(own, 1), rows)]
    offset_by = jax.random.randint(jax.random.fold_in(own, 2), (rows, 1), 0, top)
    return jnp.take_along_axis(table, (jnp.arange(top)[None, :] + offset_by) % top, axis=1)


def portions_of(count, total, limit, lean, full):
    portions = [(1 << 20) // math.isqrt(standing ** lean) + 1 for standing in range(1, count + 1)]
    largest = limit if full else min(limit, max(-(-total // count), total * portions[0] // sum(portions)))
    least = 1 if total - largest >= count - 1 else 0
    given, rest = [largest] + [least] * (count - 1), total - largest - least * (count - 1)
    while rest > 0:
        candidates = [i for i in range(1, count) if given[i] < largest] or [i for i in range(1, count) if given[i] < limit]
        whole, budget = sum([portions[i] for i in candidates]), rest
        for i in candidates:
            more = min(limit - given[i], max(1, budget * portions[i] // whole), rest)
            given[i] = given[i] + more
            rest = rest - more
    return np.array(given)


def scatter_about(key, shape, width, most, cuts=(), held_as=jnp.bfloat16):
    level = block_levels(key, shape, cuts, -0.22, 0.18) if cuts else 1.0
    values = jax.random.normal(key, shape, jnp.float32) * width * level
    return jnp.minimum(jnp.maximum(values, -most), most).astype(held_as)


def setup_inputs(seed: int = 0) -> dict:
    splits = jax.random.split(jax.random.key(seed), 11)
    field = scatter_about(splits[0], (DOFS, ELEMS), 1.0, 6.0, ((1, 128),), jnp.float32)
    edge_signs = draw_edge_signs(jax.random.fold_in(splits[10], 71), 0)
    face_nbrs = draw_face_nbrs(jax.random.fold_in(splits[10], 71), 0)
    elem_size = jnp.clip(jnp.exp(math.log(2.0) - 1.3862944 * jax.random.uniform(splits[3], (ELEMS,), jnp.float32) ** block_levels(splits[3], (ELEMS,), ((0, 128),), -0.2, 0.2)), 0.5, 2.0)
    mu_inv = jnp.clip(jnp.exp(math.log(4.0) - 2.7725887 * jax.random.uniform(splits[4], (ELEMS,), jnp.float32) ** block_levels(splits[4], (ELEMS,), ((0, 128),), -0.2, 0.2)), 0.25, 4.0)
    permittivity = jnp.clip(jnp.exp(math.log(4.0) - 2.7725887 * jax.random.uniform(splits[5], (ELEMS,), jnp.float32) ** block_levels(splits[5], (ELEMS,), ((0, 128),), -0.2, 0.2)), 0.25, 4.0)
    new_owner_keys = jax.random.split(jax.random.fold_in(splits[6], 1), ELEMS // E_DEV)
    new_owner_turns = jax.random.permutation(jax.random.fold_in(splits[6], 3), ELEMS // E_DEV)
    new_owner = jax.vmap(lambda own, number: shared_out(jax.random.fold_in(splits[6], 2), own, number, E_DEV, N_GX * N_YZ, 1, CAP, 2))(new_owner_keys, new_owner_turns).reshape((ELEMS, 1))
    trace_map = scatter_about(splits[7], (DOFS, 6 * FT), DOFS ** -0.5, 0.5, (), jnp.float32)
    stiffness = scatter_about(splits[8], (DOFS, DOFS), DOFS ** -0.5, 0.5, (), jnp.float32)
    mass = scatter_about(splits[9], (DOFS, DOFS), DOFS ** -0.5, 0.5, (), jnp.float32)
    return dict(field=field, edge_signs=edge_signs, face_nbrs=face_nbrs, elem_size=elem_size, mu_inv=mu_inv, permittivity=permittivity, new_owner=new_owner, trace_map=trace_map, stiffness=stiffness, mass=mass)


def expansion():
    table = np.zeros((12, 144), np.float32)
    for i in range(36):
        if i % 3 != 1:
            table[i // 3, i] = 1.0
    return jnp.asarray(table)

def reference(field, edge_signs, face_nbrs, elem_size, mu_inv, permittivity, new_owner, trace_map, stiffness, mass):
    hi = lax.Precision.HIGHEST
    devices = N_GX * N_YZ
    shifted = (edge_signs.T - 1).astype(jnp.float32)
    signs = 1.0 + jnp.dot(shifted, expansion(), precision=hi)
    oriented = field.T * signs
    traces = jnp.dot(oriented, trace_map, precision=hi)
    faces = traces.reshape(ELEMS * 6, FT)
    opposite = jnp.array([1, 0, 3, 2, 5, 4], jnp.int32)
    nbrs = face_nbrs.T
    valid = nbrs >= 0
    index = jnp.where(valid, nbrs * 6 + opposite[None, :], 0).astype(jnp.int32)
    across = jnp.where(valid[:, :, None], faces[index], 0.0)
    jump = traces.reshape(ELEMS, 6, FT) - across
    indicators = jnp.sqrt(elem_size * lax.optimization_barrier(jnp.mean(jump * jump, axis=(1, 2))) + 1e-06)
    owner = new_owner[:, 0].reshape(devices, E_DEV)
    targets = jnp.arange(devices, dtype=jnp.int32)

    def block_rank(row):
        onehot = (row[:, None] == targets[None, :]).astype(jnp.int32)
        return (lax.optimization_barrier(jnp.sum(onehot * jnp.cumsum(onehot, axis=0), axis=1)) - 1).astype(jnp.int32)
    rank = lax.map(block_rank, owner).reshape(ELEMS)
    source = (jnp.arange(ELEMS, dtype=jnp.int32) // E_DEV).astype(jnp.int32)
    pos = (new_owner[:, 0] * (devices * CAP) + source * CAP + rank).astype(jnp.int32)
    migrated = jnp.zeros((SLOTS, DOFS), jnp.float32).at[pos].set(oriented)
    result = mu_inv[:, None] * jnp.dot(oriented, stiffness, precision=hi) + permittivity[:, None] * jnp.dot(oriented, mass, precision=hi)
    applied = jnp.zeros((SLOTS, DOFS), jnp.float32).at[pos].set(result)
    return (indicators, migrated.T, applied.T)
```

```python
import functools

import jax
import jax.numpy as jnp
from jax import lax
from jax.experimental import pallas as pl
from jax.experimental.pallas import tpu as pltpu
from jax.sharding import PartitionSpec as P

AXES = ("gx", "yz")
LANES = 128
VMEM_LIMIT = 40 << 20


def split3(value):
    high = value.astype(jnp.bfloat16)
    low = (value - high.astype(jnp.float32)).astype(jnp.bfloat16)
    return high, low


def product3(left, right):
    dims = (((0,), (0,)), ((), ()))
    dot = functools.partial(lax.dot_general, dimension_numbers=dims, preferred_element_type=jnp.float32)
    return dot(left[0], right[0]) + (dot(left[0], right[1]) + dot(left[1], right[0]))


def lane_gather(table, index):
    return jnp.take_along_axis(table, index, axis=1)


def row8(row):
    return jnp.broadcast_to(row, (8, LANES))


def orient_kernel(field_ref, signs_ref, map_ref, oriented_ref, traces_ref):
    edges = signs_ref.shape[0]
    rows = lax.broadcasted_iota(jnp.int32, (40, edges), 0)
    edge = lax.broadcasted_iota(jnp.int32, (40, edges), 1)
    picks = ((rows < 36) & (rows % 3 != 1) & (rows // 3 == edge)).astype(jnp.bfloat16)
    shifted = (signs_ref[...] - 1).astype(jnp.float32).astype(jnp.bfloat16)
    factor = 1.0 + jnp.dot(picks, shifted, preferred_element_type=jnp.float32)
    oriented_ref[0:40, :] = field_ref[0:40, :] * factor
    oriented_ref[40:, :] = field_ref[40:, :]
    traces_ref[...] = product3(split3(map_ref[...]), split3(oriented_ref[...]))


def orient(field, edge_signs, trace_map):
    dofs, count = field.shape
    edges = edge_signs.shape[0]
    block = min(count, 512)
    return pl.pallas_call(
        orient_kernel,
        grid=(count // block,),
        in_specs=[
            pl.BlockSpec((dofs, block), lambda i: (0, i)),
            pl.BlockSpec((edges, block), lambda i: (0, i)),
            pl.BlockSpec((dofs, dofs), lambda i: (0, 0)),
        ],
        out_specs=[pl.BlockSpec((dofs, block), lambda i: (0, i))] * 2,
        out_shape=[jax.ShapeDtypeStruct((dofs, count), jnp.float32)] * 2,
        compiler_params=pltpu.CompilerParams(vmem_limit_bytes=VMEM_LIMIT),
        cost_estimate=pl.CostEstimate(flops=2 * dofs * dofs * count * 3, bytes_accessed=12 * dofs * count, transcendentals=0),
        name="orient",
    )(field, edge_signs, trace_map)


def quarter_swap(parts, lane):
    upper = (lane & 64) != 0
    odd = (lane & 32) != 0
    a0, a1, a2, a3 = parts
    b0 = jnp.where(upper, pltpu.roll(a2, 64, 1), a0)
    b2 = jnp.where(upper, a2, pltpu.roll(a0, 64, 1))
    b1 = jnp.where(upper, pltpu.roll(a3, 64, 1), a1)
    b3 = jnp.where(upper, a3, pltpu.roll(a1, 64, 1))
    c0 = jnp.where(odd, pltpu.roll(b1, 32, 1), b0)
    c1 = jnp.where(odd, b1, pltpu.roll(b0, 96, 1))
    c2 = jnp.where(odd, pltpu.roll(b3, 32, 1), b2)
    c3 = jnp.where(odd, b3, pltpu.roll(b2, 96, 1))
    return c0, c1, c2, c3


def pack_kernel(oriented_ref, scale_ref, owner_ref, payload_ref, high_ref, low_ref):
    tiles = owner_ref.shape[1] // LANES
    groups = payload_ref.shape[0] // 4
    bf = jnp.bfloat16
    sub = lax.broadcasted_iota(jnp.int32, (LANES, LANES), 0)
    lane_full = lax.broadcasted_iota(jnp.int32, (LANES, LANES), 1)
    upto = (sub <= lane_full).astype(jnp.float32).astype(bf)
    ones = jnp.ones((LANES, LANES), bf)
    before = jnp.zeros((LANES, LANES), jnp.float32)
    nt = (((1,), (1,)), ((), ()))
    table = jnp.zeros((3 * groups, LANES), jnp.float32)
    for tile in range(tiles):
        owner = owner_ref[:, tile * LANES : (tile + 1) * LANES]
        onehot = sub == owner
        hot = onehot.astype(jnp.float32)
        hot16 = hot.astype(bf)
        ordinal = before + jnp.dot(hot16, upto, preferred_element_type=jnp.float32) - 1.0
        rank = jnp.sum(jnp.where(onehot, ordinal, 0.0), axis=0, keepdims=True)
        before = before + jnp.dot(hot16, ones, preferred_element_type=jnp.float32)
        place = (owner & 3) * 32 + rank.astype(jnp.int32)
        landing = (sub == place).astype(jnp.float32).astype(bf)
        group = lax.broadcasted_iota(jnp.int32, (groups, LANES), 0) == (owner >> 2)
        groupf = group.astype(jnp.float32)
        lane_row = lax.broadcasted_iota(jnp.int32, (groups, LANES), 1).astype(jnp.float32)
        left = jnp.concatenate([groupf, groupf * lane_row, groupf * float(tile)], axis=0).astype(bf)
        table = table + lax.dot_general(left, landing, nt, preferred_element_type=jnp.float32)
    found = table[:groups]
    high_ref[...] = jnp.where(found > 0.5, table[2 * groups :], -1.0).astype(jnp.int32)
    low_ref[...] = table[groups : 2 * groups].astype(jnp.int32)

    lane = lax.broadcasted_iota(jnp.int32, (8, LANES), 1)
    rows = oriented_ref.shape[0] // 8

    def one_group(step, carry):
        high = row8(high_ref[pl.ds(step, 1), :])
        low = row8(low_ref[pl.ds(step, 1), :])
        taken = [jnp.zeros((8, LANES), jnp.float32) for _ in range(rows + 1)]
        for tile in range(tiles):
            hit = high == tile
            cols = slice(tile * LANES, (tile + 1) * LANES)
            for r in range(rows + 1):
                source = oriented_ref[8 * r : 8 * r + 8, cols] if r < rows else scale_ref[:, cols]
                taken[r] = jnp.where(hit, lane_gather(source, low), taken[r])
        taken.append(jnp.zeros((8, LANES), jnp.float32))
        for i in range(len(taken) // 4):
            outs = quarter_swap(taken[4 * i : 4 * i + 4], lane)
            for q in range(4):
                payload_ref[4 * step + q, 8 * i : 8 * i + 8, :] = outs[q]
        return carry

    lax.fori_loop(0, groups, one_group, 0)


def pack(oriented, scale, owner, devices):
    dofs, count = oriented.shape
    depth = 8 * ((dofs // 8 + 1 + 3) // 4)
    groups = devices // 4
    whole = pl.BlockSpec(memory_space=pltpu.VMEM)
    return pl.pallas_call(
        pack_kernel,
        in_specs=[whole] * 3,
        out_specs=whole,
        out_shape=jax.ShapeDtypeStruct((devices, depth, LANES), jnp.float32),
        scratch_shapes=[pltpu.VMEM((groups, LANES), jnp.int32), pltpu.VMEM((groups, LANES), jnp.int32)],
        compiler_params=pltpu.CompilerParams(vmem_limit_bytes=VMEM_LIMIT),
        cost_estimate=pl.CostEstimate(flops=10**9, bytes_accessed=8 * 10**6, transcendentals=0),
        name="pack",
    )(oriented, scale, owner)


def jump_kernel(base_ref, own_ref, left_ref, right_ref, nbrs_ref, size_ref, out_ref):
    count = own_ref.shape[1]
    tiles = count // LANES
    width = own_ref.shape[0] // 6
    vecs = width // 8
    base = base_ref[0]
    sides = (left_ref, own_ref, right_ref)

    def one_tile(step, carry):
        cols = pl.ds(pl.multiple_of(step * LANES, LANES), LANES)
        total = jnp.zeros((8, LANES), jnp.float32)
        for face in range(6):
            other = face ^ 1
            nbr = row8(nbrs_ref[face : face + 1, cols])
            spot = jnp.where(nbr >= 0, nbr - base, -LANES)
            high = spot >> 7
            low = spot & (LANES - 1)
            got = [jnp.zeros((8, LANES), jnp.float32) for _ in range(vecs)]
            for s, side in enumerate(sides):
                for tile in range(tiles):
                    hit = high == (s * tiles + tile)
                    for v in range(vecs):
                        r = other * width + 8 * v
                        source = side[r : r + 8, tile * LANES : (tile + 1) * LANES]
                        got[v] = jnp.where(hit, lane_gather(source, low), got[v])
            for v in range(vecs):
                r = face * width + 8 * v
                jump = own_ref[r : r + 8, cols] - got[v]
                total = total + jump * jump
        squares = jnp.sum(total, axis=0, keepdims=True)
        out_ref[:, cols] = jnp.sqrt(size_ref[:, cols] * (squares / (6 * width)) + 1e-06)
        return carry

    lax.fori_loop(0, tiles, one_tile, 0)


def jumps(base, own, left, right, nbrs, size):
    whole = pl.BlockSpec(memory_space=pltpu.VMEM)
    count = own.shape[1]
    return pl.pallas_call(
        jump_kernel,
        in_specs=[pl.BlockSpec(memory_space=pltpu.SMEM)] + [whole] * 5,
        out_specs=whole,
        out_shape=jax.ShapeDtypeStruct((1, count), jnp.float32),
        compiler_params=pltpu.CompilerParams(vmem_limit_bytes=VMEM_LIMIT),
        cost_estimate=pl.CostEstimate(flops=10**9, bytes_accessed=4 * 10**6, transcendentals=0),
        name="jumps",
    )(base, own, left, right, nbrs, size)


def apply_kernel(received_ref, stiffness_ref, mass_ref, migrated_ref, applied_ref, scale_ref):
    lane = lax.broadcasted_iota(jnp.int32, (8, LANES), 1)
    dofs = migrated_ref.shape[0]
    rows = dofs // 8
    for t in range(received_ref.shape[0] // 4):
        cols = slice(t * LANES, (t + 1) * LANES)
        for i in range(received_ref.shape[1] // 8):
            outs = quarter_swap([received_ref[4 * t + q, 8 * i : 8 * i + 8, :] for q in range(4)], lane)
            for q in range(4):
                r = 4 * i + q
                if r < rows:
                    migrated_ref[8 * r : 8 * r + 8, cols] = outs[q]
                elif r == rows:
                    scale_ref[:, cols] = outs[q]
    right = split3(migrated_ref[...])
    first = product3(split3(stiffness_ref[...]), right)
    second = product3(split3(mass_ref[...]), right)
    applied_ref[...] = scale_ref[0:1, :] * first + scale_ref[1:2, :] * second


def apply_received(received, stiffness, mass):
    devices, depth, _ = received.shape
    dofs = stiffness.shape[0]
    per = 16
    block = per * 32
    return pl.pallas_call(
        apply_kernel,
        grid=(devices // per,),
        in_specs=[
            pl.BlockSpec((per, depth, LANES), lambda i: (i, 0, 0)),
            pl.BlockSpec((dofs, dofs), lambda i: (0, 0)),
            pl.BlockSpec((dofs, dofs), lambda i: (0, 0)),
        ],
        out_specs=[pl.BlockSpec((dofs, block), lambda i: (0, i))] * 2,
        out_shape=[jax.ShapeDtypeStruct((dofs, devices * 32), jnp.float32)] * 2,
        scratch_shapes=[pltpu.VMEM((8, block), jnp.float32)],
        compiler_params=pltpu.CompilerParams(vmem_limit_bytes=VMEM_LIMIT),
        cost_estimate=pl.CostEstimate(flops=10**9, bytes_accessed=8 * 10**6, transcendentals=0),
        name="apply",
    )(received, stiffness, mass)


def body(field, edge_signs, face_nbrs, elem_size, mu_inv, permittivity, new_owner, trace_map, stiffness, mass):
    count = field.shape[1]
    devices = lax.axis_size(AXES)
    me = lax.axis_index(AXES)
    oriented, traces = orient(field, edge_signs, trace_map)
    left = lax.ppermute(traces, AXES, [(i, i + 1) for i in range(devices - 1)])
    right = lax.ppermute(traces, AXES, [(i + 1, i) for i in range(devices - 1)])
    scale = jnp.concatenate(
        [mu_inv.reshape(1, count), permittivity.reshape(1, count), jnp.zeros((6, count), jnp.float32)], axis=0
    )
    payload = pack(oriented, scale, new_owner.reshape(1, count), devices)
    received = lax.all_to_all(payload, AXES, split_axis=0, concat_axis=0, tiled=True)
    base = ((me - 1) * count).astype(jnp.int32).reshape(1)
    indicators = jumps(base, traces, left, right, face_nbrs, elem_size.reshape(1, count))
    migrated, applied = apply_received(received, stiffness, mass)
    return indicators.reshape(count), migrated, applied


def solution(mesh):
    flat = P(AXES)
    wide = P(None, AXES)
    in_specs = (wide, wide, wide, flat, flat, flat, P(AXES, None), P(), P(), P())
    return jax.shard_map(body, mesh=mesh, in_specs=in_specs, out_specs=(flat, wide, wide), check_vma=False)
```

```python
import functools

import jax
import jax.numpy as jnp
from jax import lax
from jax.experimental import pallas as pl
from jax.experimental.pallas import tpu as pltpu
from jax.sharding import PartitionSpec as P

AXES = ("gx", "yz")
LANES = 128
VMEM_LIMIT = 60 << 20


def split3(value):
    high = value.astype(jnp.bfloat16)
    low = (value - high.astype(jnp.float32)).astype(jnp.bfloat16)
    return high, low


def product3(left, right):
    dims = (((0,), (0,)), ((), ()))
    dot = functools.partial(lax.dot_general, dimension_numbers=dims, preferred_element_type=jnp.float32)
    return dot(left[0], right[0]) + (dot(left[0], right[1]) + dot(left[1], right[0]))


def lane_gather(table, index):
    return jnp.take_along_axis(table, index, axis=1)


def row8(row):
    return jnp.broadcast_to(row, (8, LANES))


def quarter_swap(parts, lane):
    upper = (lane & 64) != 0
    odd = (lane & 32) != 0
    a0, a1, a2, a3 = parts
    b0 = jnp.where(upper, pltpu.roll(a2, 64, 1), a0)
    b2 = jnp.where(upper, a2, pltpu.roll(a0, 64, 1))
    b1 = jnp.where(upper, pltpu.roll(a3, 64, 1), a1)
    b3 = jnp.where(upper, a3, pltpu.roll(a1, 64, 1))
    c0 = jnp.where(odd, pltpu.roll(b1, 32, 1), b0)
    c1 = jnp.where(odd, b1, pltpu.roll(b0, 96, 1))
    c2 = jnp.where(odd, pltpu.roll(b3, 32, 1), b2)
    c3 = jnp.where(odd, b3, pltpu.roll(b2, 96, 1))
    return c0, c1, c2, c3


MESH = pl.DeviceIdType.MESH
CHUNKS = 4


def bit(k, n):
    return lax.rem(lax.div(k, 2**n), 2)


def offsets(k):
    return bit(k, 1) + 2 * bit(k, 3), bit(k, 4), bit(k, 0) + 2 * bit(k, 2)


def exchange_kernel(
    field_ref, signs_ref, nbrs_ref, mu_ref, eps_ref, owner_ref, map_ref,
    squares_ref, received_ref,
    oriented, traces, left, right, signs, nbrs, mu, eps, owner, tmap, scale, high_ref, low_ref, payload, bundle,
    in_sem, halo_send, halo_recv, a_send, a_recv, f_send, f_recv, own_sem,
):
    gx = lax.axis_index("gx")
    yz = lax.axis_index("yz")
    gx_size = lax.axis_size("gx")
    yz_size = lax.axis_size("yz")
    devices = gx_size * yz_size
    me = gx * yz_size + yz
    z, c = lax.div(gx, 2), lax.rem(gx, 2)
    y, x = lax.div(yz, 4), lax.rem(yz, 4)
    plane = gx * 4 + y
    planes = devices // 4
    dofs, count = oriented.shape
    depth = payload.shape[1]
    block = count // CHUNKS

    def at(index):
        return (lax.div(index, yz_size), lax.rem(index, yz_size))

    def in_plane(p):
        return (lax.div(p, 4), lax.rem(p, 4) * 4 + x)

    def target(k):
        oz, oc, oy = offsets(k)
        return (lax.rem(z + oz, 4) * 2 + lax.rem(c + oc, 2)) * 4 + lax.rem(y + oy, 4)

    def source(k):
        oz, oc, oy = offsets(k)
        return (lax.rem(z + 4 - oz, 4) * 2 + lax.rem(c + 2 - oc, 2)) * 4 + lax.rem(y + 4 - oy, 4)

    ahead = at(lax.rem(me + 1, devices))
    behind = at(lax.rem(me + devices - 1, devices))

    loads = [
        pltpu.make_async_copy(signs_ref, signs, in_sem.at[0]),
        pltpu.make_async_copy(map_ref, tmap, in_sem.at[1]),
    ]
    fields = []
    for part in range(CHUNKS):
        cols = pl.ds(part * block, block)
        fields.append(pltpu.make_async_copy(field_ref.at[:, cols], oriented.at[:, cols], in_sem.at[2 + part]))
    later = [
        pltpu.make_async_copy(s, d, in_sem.at[2 + CHUNKS + i])
        for i, (s, d) in enumerate(((owner_ref, owner), (mu_ref, mu), (eps_ref, eps), (nbrs_ref, nbrs)))
    ]
    for copy in loads + fields + later:
        copy.start()

    barrier = pltpu.get_barrier_semaphore()

    def greet(k, carry):
        pl.semaphore_signal(barrier, inc=1, device_id=in_plane(target(k)), device_id_type=MESH)
        return carry

    lax.fori_loop(1, planes, greet, 0)
    for step in range(1, 4):
        pl.semaphore_signal(barrier, inc=1, device_id=(gx, y * 4 + lax.rem(x + step, 4)), device_id_type=MESH)
    pl.semaphore_signal(barrier, inc=1, device_id=ahead, device_id_type=MESH)
    pl.semaphore_signal(barrier, inc=1, device_id=behind, device_id_type=MESH)

    edges = signs.shape[0]
    rows = lax.broadcasted_iota(jnp.int32, (40, edges), 0)
    edge = lax.broadcasted_iota(jnp.int32, (40, edges), 1)
    picks = ((rows < 36) & (rows % 3 != 1) & (rows // 3 == edge)).astype(jnp.bfloat16)

    def halo(part):
        cols = pl.ds(part * block, block)
        return [
            pltpu.make_async_remote_copy(
                src_ref=traces.at[:, cols], dst_ref=side.at[:, cols], send_sem=halo_send.at[i, part],
                recv_sem=halo_recv.at[i, part], device_id=peer, device_id_type=MESH,
            )
            for i, (side, peer) in enumerate(((left, ahead), (right, behind)))
        ]

    for copy in loads:
        copy.wait()
    map_parts = split3(tmap[...])
    for part in range(CHUNKS):
        cols = slice(part * block, (part + 1) * block)
        fields[part].wait()
        shifted = (signs[:, cols] - 1).astype(jnp.float32).astype(jnp.bfloat16)
        factor = 1.0 + jnp.dot(picks, shifted, preferred_element_type=jnp.float32)
        oriented[0:40, cols] = oriented[0:40, cols] * factor
        traces[:, cols] = product3(map_parts, split3(oriented[:, cols]))
        if part == 1:
            pl.semaphore_wait(barrier, planes - 1 + 3 + 2)
        if part >= 1:
            for copy in halo(part - 1):
                copy.start()
    for copy in later:
        copy.wait()

    tiles = count // LANES
    bf = jnp.bfloat16
    sub = lax.broadcasted_iota(jnp.int32, (LANES, LANES), 0)
    lane_full = lax.broadcasted_iota(jnp.int32, (LANES, LANES), 1)
    upto = (sub <= lane_full).astype(jnp.float32).astype(bf)
    ones = jnp.ones((LANES, LANES), bf)
    before = jnp.zeros((LANES, LANES), jnp.float32)
    nt = (((1,), (1,)), ((), ()))
    table = jnp.zeros((3 * planes, LANES), jnp.float32)
    sub8 = lax.broadcasted_iota(jnp.int32, (8, LANES), 0)
    for tile in range(tiles):
        cols = slice(tile * LANES, (tile + 1) * LANES)
        scale[:, cols] = jnp.where(sub8 == 0, row8(mu[:, cols]), jnp.where(sub8 == 1, row8(eps[:, cols]), 0.0))
        own = owner[:, cols]
        onehot = sub == own
        hot = onehot.astype(jnp.float32)
        hot16 = hot.astype(bf)
        ordinal = before + jnp.dot(hot16, upto, preferred_element_type=jnp.float32) - 1.0
        rank = jnp.sum(jnp.where(onehot, ordinal, 0.0), axis=0, keepdims=True)
        before = before + jnp.dot(hot16, ones, preferred_element_type=jnp.float32)
        place = (own & 3) * 32 + rank.astype(jnp.int32)
        landing = (sub == place).astype(jnp.float32).astype(bf)
        group = lax.broadcasted_iota(jnp.int32, (planes, LANES), 0) == (own >> 2)
        groupf = group.astype(jnp.float32)
        lane_row = lax.broadcasted_iota(jnp.int32, (planes, LANES), 1).astype(jnp.float32)
        parts = jnp.concatenate([groupf, groupf * lane_row, groupf * float(tile)], axis=0).astype(bf)
        table = table + lax.dot_general(parts, landing, nt, preferred_element_type=jnp.float32)
    found = table[:planes]
    high_ref[...] = jnp.where(found > 0.5, table[2 * planes :], -1.0).astype(jnp.int32)
    low_ref[...] = table[planes : 2 * planes].astype(jnp.int32)
    for copy in halo(CHUNKS - 1):
        copy.start()

    lane = lax.broadcasted_iota(jnp.int32, (8, LANES), 1)
    vectors = dofs // 8

    def pack_group(k):
        t = target(k)
        high = row8(high_ref[pl.ds(t, 1), :])
        low = row8(low_ref[pl.ds(t, 1), :])
        taken = [jnp.zeros((8, LANES), jnp.float32) for _ in range(vectors + 1)]
        for tile in range(tiles):
            hit = high == tile
            cols = slice(tile * LANES, (tile + 1) * LANES)
            for r in range(vectors + 1):
                piece = oriented[8 * r : 8 * r + 8, cols] if r < vectors else scale[:, cols]
                taken[r] = jnp.where(hit, lane_gather(piece, low), taken[r])
        while len(taken) % 4:
            taken.append(jnp.zeros((8, LANES), jnp.float32))
        for i in range(len(taken) // 4):
            outs = quarter_swap(taken[4 * i : 4 * i + 4], lane)
            for q in range(4):
                payload[4 * t + q, 8 * i : 8 * i + 8, :] = outs[q]

    def send_group(k):
        t = target(k)
        pltpu.make_async_remote_copy(
            src_ref=payload.at[pl.ds(4 * t, 4)], dst_ref=bundle.at[pl.ds(4 * plane, 4)], send_sem=a_send,
            recv_sem=a_recv.at[plane], device_id=in_plane(t), device_id_type=MESH,
        ).start()

    def pack_step(k, carry):
        pack_group(k)

        @pl.when(k > 1)
        def _():
            send_group(k - 1)

        return carry

    lax.fori_loop(1, planes, pack_step, 0)
    pack_group(0)
    send_group(planes - 1)

    def forward(origin, s):
        for step in range(1, 4):
            xd = lax.rem(x + step, 4)
            pltpu.make_async_remote_copy(
                src_ref=origin.at[4 * s + xd], dst_ref=received_ref.at[4 * s + x], send_sem=f_send, recv_sem=f_recv,
                device_id=(gx, y * 4 + xd), device_id_type=MESH,
            ).start()
        pltpu.make_async_copy(origin.at[4 * s + x], received_ref.at[4 * s + x], own_sem).start()

    def forward_step(k):
        s = source(k)
        pltpu.make_async_remote_copy(
            src_ref=payload.at[pl.ds(4 * s, 4)], dst_ref=bundle.at[pl.ds(4 * s, 4)], send_sem=a_send,
            recv_sem=a_recv.at[s], device_id=ahead, device_id_type=MESH,
        ).wait_recv()
        forward(bundle, s)

    early = planes // 2 + 1

    def early_step(k, carry):
        forward_step(k)
        return carry

    lax.fori_loop(1, early, early_step, 0)
    forward(payload, plane)

    for part in range(CHUNKS):
        for copy in halo(part):
            copy.wait_recv()

    width = dofs // 6
    vecs = width // 8
    base = (me - 1) * count
    sides = (left, traces, right)

    def jump_tile(step, carry):
        @pl.when(step + early < planes)
        def _():
            forward_step(step + early)

        cols = pl.ds(pl.multiple_of(step * LANES, LANES), LANES)
        total = jnp.zeros((8, LANES), jnp.float32)
        for face in range(6):
            other = face ^ 1
            nbr = row8(nbrs[face : face + 1, cols])
            spot = jnp.where(nbr >= 0, nbr - base, -LANES)
            high = spot >> 7
            low = spot & (LANES - 1)
            got = [jnp.zeros((8, LANES), jnp.float32) for _ in range(vecs)]
            for i, side in enumerate(sides):
                for tile in range(tiles):
                    hit = high == (i * tiles + tile)
                    for v in range(vecs):
                        r = other * width + 8 * v
                        piece = side[r : r + 8, tile * LANES : (tile + 1) * LANES]
                        got[v] = jnp.where(hit, lane_gather(piece, low), got[v])
            for v in range(vecs):
                r = face * width + 8 * v
                jump = traces[r : r + 8, cols] - got[v]
                total = total + jump * jump
        squares_ref[:, cols] = jnp.sum(total, axis=0, keepdims=True)
        return carry

    lax.fori_loop(0, tiles, jump_tile, 0)

    for part in range(CHUNKS):
        for copy in halo(part):
            copy.wait_send()
    sent = 4 * (planes - 1)
    pltpu.make_async_remote_copy(
        src_ref=payload.at[pl.ds(0, sent)], dst_ref=bundle.at[pl.ds(0, sent)], send_sem=a_send, recv_sem=a_recv.at[0],
        device_id=ahead, device_id_type=MESH,
    ).wait_send()
    moved = 3 * planes
    along = pltpu.make_async_remote_copy(
        src_ref=bundle.at[pl.ds(0, moved)], dst_ref=received_ref.at[pl.ds(0, moved)], send_sem=f_send, recv_sem=f_recv,
        device_id=ahead, device_id_type=MESH,
    )
    along.wait_send()
    along.wait_recv()
    pltpu.make_async_copy(bundle.at[pl.ds(0, planes)], received_ref.at[pl.ds(0, planes)], own_sem).wait()


def exchange(field, edge_signs, face_nbrs, mu, eps, owner, trace_map, devices):
    dofs, count = field.shape
    planes = devices // 4
    depth = 8 * ((dofs // 8 + 1 + 3) // 4)
    anywhere = pl.BlockSpec(memory_space=pl.ANY)
    wide = pltpu.VMEM((dofs, count), jnp.float32)
    blocks = pltpu.VMEM((devices, depth, LANES), jnp.float32)
    row = pltpu.VMEM((1, count), jnp.float32)
    dma = pltpu.SemaphoreType.DMA
    return pl.pallas_call(
        exchange_kernel,
        in_specs=[anywhere] * 7,
        out_specs=[pl.BlockSpec(memory_space=pltpu.VMEM), anywhere],
        out_shape=[
            jax.ShapeDtypeStruct((1, count), jnp.float32),
            jax.ShapeDtypeStruct((devices, depth, LANES), jnp.float32),
        ],
        scratch_shapes=[
            wide, wide, wide, wide,
            pltpu.VMEM(edge_signs.shape, jnp.int32),
            pltpu.VMEM(face_nbrs.shape, jnp.int32),
            row, row, pltpu.VMEM((1, count), jnp.int32),
            pltpu.VMEM(trace_map.shape, jnp.float32),
            pltpu.VMEM((8, count), jnp.float32),
            pltpu.VMEM((planes, LANES), jnp.int32),
            pltpu.VMEM((planes, LANES), jnp.int32),
            blocks, blocks,
            dma((CHUNKS + 6,)), dma((2, CHUNKS)), dma((2, CHUNKS)), dma, dma((planes,)), dma, dma, dma,
        ],
        compiler_params=pltpu.CompilerParams(collective_id=0, has_side_effects=True, vmem_limit_bytes=VMEM_LIMIT),
        name="exchange",
    )(field, edge_signs, face_nbrs, mu, eps, owner, trace_map)


def apply_kernel(
    received_ref, stiffness_ref, mass_ref, squares_ref, size_ref, migrated_ref, applied_ref, out_ref, scale_ref
):
    @pl.when(pl.program_id(0) == 0)
    def _():
        out_ref[...] = jnp.sqrt(size_ref[...] * (squares_ref[...] / stiffness_ref.shape[0]) + 1e-06)

    lane = lax.broadcasted_iota(jnp.int32, (8, LANES), 1)
    dofs = migrated_ref.shape[0]
    rows = dofs // 8
    for t in range(received_ref.shape[0] // 4):
        cols = slice(t * LANES, (t + 1) * LANES)
        for i in range(received_ref.shape[1] // 8):
            outs = quarter_swap([received_ref[4 * t + q, 8 * i : 8 * i + 8, :] for q in range(4)], lane)
            for q in range(4):
                r = 4 * i + q
                if r < rows:
                    migrated_ref[8 * r : 8 * r + 8, cols] = outs[q]
                elif r == rows:
                    scale_ref[:, cols] = outs[q]
    right = split3(migrated_ref[...])
    first = product3(split3(stiffness_ref[...]), right)
    second = product3(split3(mass_ref[...]), right)
    applied_ref[...] = scale_ref[0:1, :] * first + scale_ref[1:2, :] * second


def apply_received(received, stiffness, mass, squares, size):
    devices, depth, _ = received.shape
    dofs = stiffness.shape[0]
    per = 16
    block = per * 32
    return pl.pallas_call(
        apply_kernel,
        grid=(devices // per,),
        in_specs=[
            pl.BlockSpec((per, depth, LANES), lambda i: (i, 0, 0)),
            pl.BlockSpec((dofs, dofs), lambda i: (0, 0)),
            pl.BlockSpec((dofs, dofs), lambda i: (0, 0)),
            pl.BlockSpec(squares.shape, lambda i: (0, 0)),
            pl.BlockSpec(squares.shape, lambda i: (0, 0)),
        ],
        out_specs=[pl.BlockSpec((dofs, block), lambda i: (0, i))] * 2 + [pl.BlockSpec(squares.shape, lambda i: (0, 0))],
        out_shape=[jax.ShapeDtypeStruct((dofs, devices * 32), jnp.float32)] * 2
        + [jax.ShapeDtypeStruct(squares.shape, jnp.float32)],
        scratch_shapes=[pltpu.VMEM((8, block), jnp.float32)],
        compiler_params=pltpu.CompilerParams(vmem_limit_bytes=VMEM_LIMIT),
        cost_estimate=pl.CostEstimate(flops=10**9, bytes_accessed=8 * 10**6, transcendentals=0),
        name="apply",
    )(received, stiffness, mass, squares, size)


def body(field, edge_signs, face_nbrs, elem_size, mu_inv, permittivity, new_owner, trace_map, stiffness, mass):
    count = field.shape[1]
    devices = lax.axis_size(AXES)
    row = (1, count)
    squares, received = exchange(
        field, edge_signs, face_nbrs, mu_inv.reshape(row), permittivity.reshape(row), new_owner.reshape(row),
        trace_map, devices,
    )
    migrated, applied, indicators = apply_received(received, stiffness, mass, squares, elem_size.reshape(row))
    return indicators.reshape(count), migrated, applied


def solution(mesh):
    flat = P(AXES)
    wide = P(None, AXES)
    in_specs = (wide, wide, wide, flat, flat, flat, P(AXES, None), P(), P(), P())
    return jax.shard_map(body, mesh=mesh, in_specs=in_specs, out_specs=(flat, wide, wide), check_vma=False)
```

```python
import functools

import jax
import jax.numpy as jnp
from jax import lax
from jax.experimental import pallas as pl
from jax.experimental.pallas import tpu as pltpu
from jax.sharding import PartitionSpec as P

AXES = ("gx", "yz")
LANES = 128
VMEM_LIMIT = 60 << 20


def split3(value):
    high = value.astype(jnp.bfloat16)
    low = (value - high.astype(jnp.float32)).astype(jnp.bfloat16)
    return high, low


def stacked_left(matrix):
    high, low = split3(jnp.transpose(matrix))
    return jnp.concatenate([high, high, low], axis=1)


def stacked_product(left, right):
    high, low = split3(right)
    return jnp.dot(left, jnp.concatenate([high, low, high], axis=0), preferred_element_type=jnp.float32)


def lane_gather(table, index):
    return jnp.take_along_axis(table, index, axis=1)


def row8(row):
    return jnp.broadcast_to(row, (8, LANES))


def quarter_swap(parts, lane):
    upper = (lane & 64) != 0
    odd = (lane & 32) != 0
    a0, a1, a2, a3 = parts
    b0 = jnp.where(upper, pltpu.roll(a2, 64, 1), a0)
    b2 = jnp.where(upper, a2, pltpu.roll(a0, 64, 1))
    b1 = jnp.where(upper, pltpu.roll(a3, 64, 1), a1)
    b3 = jnp.where(upper, a3, pltpu.roll(a1, 64, 1))
    c0 = jnp.where(odd, pltpu.roll(b1, 32, 1), b0)
    c1 = jnp.where(odd, b1, pltpu.roll(b0, 96, 1))
    c2 = jnp.where(odd, pltpu.roll(b3, 32, 1), b2)
    c3 = jnp.where(odd, b3, pltpu.roll(b2, 96, 1))
    return c0, c1, c2, c3


MESH = pl.DeviceIdType.MESH
CHUNKS = 4
MATRIX_FACES = (0, 1, 3, 5)


def bit(k, n):
    return lax.rem(lax.div(k, 2**n), 2)


def offsets(k):
    return bit(k, 1) + 2 * bit(k, 3), bit(k, 4), bit(k, 0) + 2 * bit(k, 2)


def exchange_kernel(
    field_ref, signs_ref, nbrs_ref, mu_ref, eps_ref, owner_ref, map_ref, stiffness_ref, mass_ref,
    squares_ref, received_ref, both_ref,
    oriented, traces, halo_traces, halo_nbrs, signs, nbrs, mu, eps, owner, tmap, scale, high_ref, low_ref, payload, bundle,
    reply_out, reply_in, own_parts, halo_parts, columns, picks_ref, matrices, both,
    in_sem, halo_send, halo_recv, a_send, a_recv, f_send, f_recv, own_sem, reply_send, reply_recv, both_sem,
):
    gx = lax.axis_index("gx")
    yz = lax.axis_index("yz")
    gx_size = lax.axis_size("gx")
    yz_size = lax.axis_size("yz")
    devices = gx_size * yz_size
    me = gx * yz_size + yz
    z, c = lax.div(gx, 2), lax.rem(gx, 2)
    y, x = lax.div(yz, 4), lax.rem(yz, 4)
    plane = gx * 4 + y
    planes = devices // 4
    dofs, count = oriented.shape
    depth = payload.shape[1]
    block = count // CHUNKS

    def at(index):
        return (lax.div(index, yz_size), lax.rem(index, yz_size))

    def in_plane(p):
        return (lax.div(p, 4), lax.rem(p, 4) * 4 + x)

    def target(k):
        oz, oc, oy = offsets(k)
        return (lax.rem(z + oz, 4) * 2 + lax.rem(c + oc, 2)) * 4 + lax.rem(y + oy, 4)

    def source(k):
        oz, oc, oy = offsets(k)
        return (lax.rem(z + 4 - oz, 4) * 2 + lax.rem(c + 2 - oc, 2)) * 4 + lax.rem(y + 4 - oy, 4)

    following = lax.rem(me + 1, devices)
    preceding = lax.rem(me + devices - 1, devices)
    ahead, behind = at(following), at(preceding)
    up_index = jnp.where(c == 0, preceding, following)
    down_index = jnp.where(c == 0, following, preceding)
    up, down = at(up_index), at(down_index)
    sink = (c == 1) & (yz == 0)
    source_end = (c == 0) & (yz == 0)
    halo_count = jnp.where(sink, 2, jnp.where(source_end, 0, 1))
    landing_slot = jnp.where((c == 0) & (yz == yz_size - 1), 1, 0)
    reply_slot = jnp.where((c == 1) & (yz == yz_size - 1), 1, 0)

    loads = [
        pltpu.make_async_copy(signs_ref, signs, in_sem.at[0]),
        pltpu.make_async_copy(map_ref, tmap, in_sem.at[1]),
    ]
    fields = []
    for part in range(CHUNKS):
        cols = pl.ds(part * block, block)
        fields.append(pltpu.make_async_copy(field_ref.at[:, cols], oriented.at[:, cols], in_sem.at[2 + part]))
    later = [
        pltpu.make_async_copy(s, d, in_sem.at[2 + CHUNKS + i])
        for i, (s, d) in enumerate(
            (
                (owner_ref, owner), (mu_ref, mu), (eps_ref, eps), (nbrs_ref, nbrs),
                (stiffness_ref, matrices.at[0]), (mass_ref, matrices.at[1]),
            )
        )
    ]
    for copy in loads + fields + later:
        copy.start()

    barrier = pltpu.get_barrier_semaphore()

    def greet(k, carry):
        pl.semaphore_signal(barrier, inc=1, device_id=in_plane(target(k)), device_id_type=MESH)
        return carry

    lax.fori_loop(1, planes, greet, 0)
    for step in range(1, 4):
        pl.semaphore_signal(barrier, inc=1, device_id=(gx, y * 4 + lax.rem(x + step, 4)), device_id_type=MESH)
    pl.semaphore_signal(barrier, inc=1, device_id=ahead, device_id_type=MESH)
    pl.semaphore_signal(barrier, inc=1, device_id=behind, device_id_type=MESH)

    edges = signs.shape[0]
    rows = lax.broadcasted_iota(jnp.int32, (40, edges), 0)
    edge = lax.broadcasted_iota(jnp.int32, (40, edges), 1)
    picks = ((rows < 36) & (rows % 3 != 1) & (rows // 3 == edge)).astype(jnp.bfloat16)

    def halo_copy(part, lane_of, slot, peer):
        cols = pl.ds(part * block, block)
        if part == CHUNKS:
            src, dst = nbrs, halo_nbrs.at[slot]
        else:
            src, dst = traces.at[:, cols], halo_traces.at[slot, :, cols]
        return pltpu.make_async_remote_copy(
            src_ref=src, dst_ref=dst, send_sem=halo_send.at[lane_of, part], recv_sem=halo_recv.at[slot, part],
            device_id=peer, device_id_type=MESH,
        )

    def halo_start(part):
        @pl.when(jnp.logical_not(sink))
        def _():
            halo_copy(part, 0, landing_slot, down).start()

        @pl.when(source_end)
        def _():
            halo_copy(part, 1, 0, up).start()

    for copy in loads:
        copy.wait()
    map_parts = stacked_left(tmap[...])
    for part in range(CHUNKS):
        cols = slice(part * block, (part + 1) * block)
        fields[part].wait()
        shifted = (signs[:, cols] - 1).astype(jnp.float32).astype(jnp.bfloat16)
        factor = 1.0 + jnp.dot(picks, shifted, preferred_element_type=jnp.float32)
        oriented[0:40, cols] = oriented[0:40, cols] * factor
        traces[:, cols] = stacked_product(map_parts, oriented[:, cols])
        if part == 1:
            pl.semaphore_wait(barrier, planes - 1 + 3 + 2)
        if part >= 1:
            halo_start(part - 1)
    for copy in later:
        copy.wait()
    halo_start(CHUNKS)

    tiles = count // LANES
    bf = jnp.bfloat16
    sub = lax.broadcasted_iota(jnp.int32, (LANES, LANES), 0)
    lane_full = lax.broadcasted_iota(jnp.int32, (LANES, LANES), 1)
    upto = (sub <= lane_full).astype(jnp.float32).astype(bf)
    ones = jnp.ones((LANES, LANES), bf)
    before = jnp.zeros((LANES, LANES), jnp.float32)
    nt = (((1,), (1,)), ((), ()))
    table = jnp.zeros((3 * planes, LANES), jnp.float32)
    sub8 = lax.broadcasted_iota(jnp.int32, (8, LANES), 0)
    for tile in range(tiles):
        cols = slice(tile * LANES, (tile + 1) * LANES)
        scale[:, cols] = jnp.where(sub8 == 0, row8(mu[:, cols]), jnp.where(sub8 == 1, row8(eps[:, cols]), 0.0))
        own = owner[:, cols]
        onehot = sub == own
        hot = onehot.astype(jnp.float32)
        hot16 = hot.astype(bf)
        ordinal = before + jnp.dot(hot16, upto, preferred_element_type=jnp.float32) - 1.0
        rank = jnp.sum(jnp.where(onehot, ordinal, 0.0), axis=0, keepdims=True)
        before = before + jnp.dot(hot16, ones, preferred_element_type=jnp.float32)
        place = (own & 3) * 32 + rank.astype(jnp.int32)
        landing = (sub == place).astype(jnp.float32).astype(bf)
        group = lax.broadcasted_iota(jnp.int32, (planes, LANES), 0) == (own >> 2)
        groupf = group.astype(jnp.float32)
        lane_row = lax.broadcasted_iota(jnp.int32, (planes, LANES), 1).astype(jnp.float32)
        parts = jnp.concatenate([groupf, groupf * lane_row, groupf * float(tile)], axis=0).astype(bf)
        table = table + lax.dot_general(parts, landing, nt, preferred_element_type=jnp.float32)
    found = table[:planes]
    high_ref[...] = jnp.where(found > 0.5, table[2 * planes :], -1.0).astype(jnp.int32)
    low_ref[...] = table[planes : 2 * planes].astype(jnp.int32)
    halo_start(CHUNKS - 1)

    lane = lax.broadcasted_iota(jnp.int32, (8, LANES), 1)
    pair = 2 * LANES
    sub_pair = lax.broadcasted_iota(jnp.int32, (LANES, pair), 0)
    height = 4 * depth
    for part in range(CHUNKS):
        cols = slice(part * block, (part + 1) * block)
        filler = jnp.zeros((height - dofs - 8, block), jnp.float32)
        value = jnp.concatenate([oriented[:, cols], scale[:, cols], filler], axis=0)
        columns[0:height, cols], columns[height:, cols] = split3(value)

    def pack_pair(k):
        two = (target(k), target(k + 1))
        high = jnp.concatenate([high_ref[pl.ds(t, 1), :] for t in two], axis=1)
        low = jnp.concatenate([low_ref[pl.ds(t, 1), :] for t in two], axis=1)
        pick = (sub_pair == low).astype(jnp.float32).astype(bf)
        for tile in range(tiles):
            gate = jnp.broadcast_to((high == tile).astype(jnp.float32), (16, pair)).astype(bf)
            picks_ref[tile * LANES : (tile + 1) * LANES, :] = pick * jnp.concatenate([gate] * 8, axis=0)
        found = jnp.dot(columns[...], picks_ref[...], preferred_element_type=jnp.float32)
        value = found[:height] + found[height:]
        for h, t in enumerate(two):
            lanes = slice(h * LANES, (h + 1) * LANES)
            for i in range(depth // 8):
                outs = quarter_swap([value[32 * i + 8 * q : 32 * i + 8 * q + 8, lanes] for q in range(4)], lane)
                for q in range(4):
                    payload[4 * t + q, 8 * i : 8 * i + 8, :] = outs[q]

    def send_group(k):
        t = target(k)
        pltpu.make_async_remote_copy(
            src_ref=payload.at[pl.ds(4 * t, 4)], dst_ref=bundle.at[pl.ds(4 * plane, 4)], send_sem=a_send,
            recv_sem=a_recv.at[plane], device_id=in_plane(t), device_id_type=MESH,
        ).start()

    def forward(origin, s):
        for step in range(1, 4):
            xd = lax.rem(x + step, 4)
            pltpu.make_async_remote_copy(
                src_ref=origin.at[4 * s + xd], dst_ref=received_ref.at[4 * s + x], send_sem=f_send, recv_sem=f_recv,
                device_id=(gx, y * 4 + xd), device_id_type=MESH,
            ).start()
        pltpu.make_async_copy(origin.at[4 * s + x], received_ref.at[4 * s + x], own_sem).start()

    def forward_step(k):
        s = source(k)
        pltpu.make_async_remote_copy(
            src_ref=payload.at[pl.ds(4 * s, 4)], dst_ref=bundle.at[pl.ds(4 * s, 4)], send_sem=a_send,
            recv_sem=a_recv.at[s], device_id=ahead, device_id_type=MESH,
        ).wait_recv()
        forward(bundle, s)

    lag = 6

    def pack_step(m, carry):
        pack_pair(2 * m)

        @pl.when(m == 1)
        def _():
            forward(payload, plane)

        @pl.when(m > 1)
        def _():
            send_group(2 * m - 2)

        @pl.when(m > 0)
        def _():
            send_group(2 * m - 1)

        @pl.when(m >= lag)
        def _():
            forward_step(m - lag + 1)

        return carry

    lax.fori_loop(0, planes // 2, pack_step, 0)
    send_group(planes - 2)
    send_group(planes - 1)
    done = planes // 2 - lag + 1

    width = dofs // 6
    vecs = width // 8

    def split_table(table, out):
        for o, odd in enumerate(MATRIX_FACES):
            rows_o = slice(odd * width, (odd + 1) * width)
            for tile in range(0, tiles, 2):
                stacked = jnp.concatenate(
                    [table[rows_o, (tile + i) * LANES : (tile + i + 1) * LANES] for i in range(2)], axis=0
                )
                high, low = split3(stacked)
                out[o, tile * width : (tile + 2) * width, 0:LANES] = high
                out[o, tile * width : (tile + 2) * width, LANES:] = low

    def jump_tile(step, faces, face_nbrs, table, parts, base, alone):
        cols = pl.ds(pl.multiple_of(step * pair, pair), pair)
        total = jnp.zeros((8, pair), jnp.float32)
        for face in range(6):
            other = face ^ 1
            nbr = jnp.broadcast_to(face_nbrs[face : face + 1, cols], (8, pair))
            spot = nbr - base
            high = spot >> 7
            low = spot & (LANES - 1)
            if other in MATRIX_FACES:
                pick = (sub_pair == low[0:1]).astype(jnp.float32).astype(jnp.bfloat16)
                found = jnp.dot(
                    parts[MATRIX_FACES.index(other)], jnp.concatenate([pick, pick], axis=0), preferred_element_type=jnp.float32
                )
                got = [jnp.zeros((8, pair), jnp.float32) for _ in range(vecs)]
                for tile in range(tiles):
                    hit = high == tile
                    for v in range(vecs):
                        r = tile * width + 8 * v
                        got[v] = jnp.where(hit, found[r : r + 8], got[v])
            else:
                halves = []
                for h in range(2):
                    lanes = slice(h * LANES, (h + 1) * LANES)
                    half = [jnp.zeros((8, LANES), jnp.float32) for _ in range(vecs)]
                    for tile in range(tiles):
                        hit = high[:, lanes] == tile
                        for v in range(vecs):
                            r = other * width + 8 * v
                            piece = table[r : r + 8, tile * LANES : (tile + 1) * LANES]
                            half[v] = jnp.where(hit, lane_gather(piece, low[:, lanes]), half[v])
                    halves.append(half)
                got = [jnp.concatenate([halves[0][v], halves[1][v]], axis=1) for v in range(vecs)]
            here = (spot >= 0) & (spot < count)
            if alone:
                here = here | (nbr < 0)
            for v in range(vecs):
                r = face * width + 8 * v
                jump = faces[r : r + 8, cols] - got[v]
                total = total + jnp.where(here, jump * jump, 0.0)
        return cols, jnp.sum(total, axis=0, keepdims=True)

    own_base = me * count

    for i in range(2):
        both[dofs * i : dofs * (i + 1)] = stacked_left(matrices[i])
    hand_over = pltpu.make_async_copy(both, both_ref, both_sem)
    split_table(traces, own_parts)

    hand_over.start()

    def own_step(step, carry):
        forward_step(done + step)
        cols, row = jump_tile(step, traces, nbrs, traces, own_parts, own_base, True)
        squares_ref[:, cols] = row
        return carry

    lax.fori_loop(0, tiles // 2, own_step, 0)
    rest = done + tiles // 2

    def halo_step(i, carry):
        for part in range(CHUNKS + 1):
            halo_copy(part, 0, i, up).wait_recv()
        base = jnp.where(i == 0, up_index, down_index) * count
        split_table(halo_traces.at[i], halo_parts)

        def across(step, inner):
            first = rest + jnp.where(sink, i * (tiles // 2) + step, 2 * step)
            second = rest + 2 * step + 1

            @pl.when(first < planes)
            def _():
                forward_step(first)

            @pl.when(jnp.logical_not(sink) & (second < planes))
            def _():
                forward_step(second)

            cols, row = jump_tile(step, traces, nbrs, halo_traces.at[i], halo_parts, base, False)
            squares_ref[:, cols] = squares_ref[:, cols] + row
            cols, row = jump_tile(step, halo_traces.at[i], halo_nbrs.at[i], traces, own_parts, own_base, False)
            reply_out[i, :, cols] = row
            return inner

        lax.fori_loop(0, tiles // 2, across, 0)
        return carry

    lax.fori_loop(0, halo_count, halo_step, 0)

    @pl.when(source_end)
    def _():
        def remaining(k, carry):
            forward_step(k)
            return carry

        lax.fori_loop(rest, planes, remaining, 0)

    def reply(slot, landing, peer):
        return pltpu.make_async_remote_copy(
            src_ref=reply_out.at[slot], dst_ref=reply_in.at[landing], send_sem=reply_send.at[slot],
            recv_sem=reply_recv.at[landing], device_id=peer, device_id_type=MESH,
        )

    @pl.when(jnp.logical_not(source_end))
    def _():
        reply(0, reply_slot, up).start()

    @pl.when(sink)
    def _():
        reply(1, 0, down).start()

    @pl.when(jnp.logical_not(sink))
    def _():
        reply(0, 0, up).wait_recv()
        squares_ref[...] = squares_ref[...] + reply_in[0]

    @pl.when(source_end)
    def _():
        reply(0, 1, up).wait_recv()
        squares_ref[...] = squares_ref[...] + reply_in[1]

    hand_over.wait()
    @pl.when(jnp.logical_not(source_end))
    def _():
        reply(0, reply_slot, up).wait_send()

    @pl.when(sink)
    def _():
        reply(1, 0, down).wait_send()

    for part in range(CHUNKS + 1):

        @pl.when(jnp.logical_not(sink))
        def _():
            halo_copy(part, 0, landing_slot, down).wait_send()

        @pl.when(source_end)
        def _():
            halo_copy(part, 1, 0, up).wait_send()

    sent = 4 * (planes - 1)
    pltpu.make_async_remote_copy(
        src_ref=payload.at[pl.ds(0, sent)], dst_ref=bundle.at[pl.ds(0, sent)], send_sem=a_send, recv_sem=a_recv.at[0],
        device_id=ahead, device_id_type=MESH,
    ).wait_send()
    moved = 3 * planes
    along = pltpu.make_async_remote_copy(
        src_ref=bundle.at[pl.ds(0, moved)], dst_ref=received_ref.at[pl.ds(0, moved)], send_sem=f_send, recv_sem=f_recv,
        device_id=ahead, device_id_type=MESH,
    )
    along.wait_send()
    along.wait_recv()
    pltpu.make_async_copy(bundle.at[pl.ds(0, planes)], received_ref.at[pl.ds(0, planes)], own_sem).wait()


def exchange(field, edge_signs, face_nbrs, mu, eps, owner, trace_map, stiffness, mass, devices):
    dofs, count = field.shape
    planes = devices // 4
    depth = 8 * ((dofs // 8 + 1 + 3) // 4)
    anywhere = pl.BlockSpec(memory_space=pl.ANY)
    wide = pltpu.VMEM((dofs, count), jnp.float32)
    blocks = pltpu.VMEM((devices, depth, LANES), jnp.float32)
    row = pltpu.VMEM((1, count), jnp.float32)
    parts = pltpu.VMEM((len(MATRIX_FACES), count // LANES * dofs // 6, 2 * LANES), jnp.bfloat16)
    dma = pltpu.SemaphoreType.DMA
    return pl.pallas_call(
        exchange_kernel,
        in_specs=[anywhere] * 9,
        out_specs=[pl.BlockSpec(memory_space=pltpu.VMEM), anywhere, anywhere],
        out_shape=[
            jax.ShapeDtypeStruct((1, count), jnp.float32),
            jax.ShapeDtypeStruct((devices, depth, LANES), jnp.float32),
            jax.ShapeDtypeStruct((2 * dofs, 3 * dofs), jnp.bfloat16),
        ],
        scratch_shapes=[
            wide, wide, pltpu.VMEM((2, dofs, count), jnp.float32), pltpu.VMEM((2, *face_nbrs.shape), jnp.int32),
            pltpu.VMEM(edge_signs.shape, jnp.int32),
            pltpu.VMEM(face_nbrs.shape, jnp.int32),
            row, row, pltpu.VMEM((1, count), jnp.int32),
            pltpu.VMEM(trace_map.shape, jnp.float32),
            pltpu.VMEM((8, count), jnp.float32),
            pltpu.VMEM((planes, LANES), jnp.int32),
            pltpu.VMEM((planes, LANES), jnp.int32),
            blocks, blocks,
            pltpu.VMEM((2, 1, count), jnp.float32), pltpu.VMEM((2, 1, count), jnp.float32), parts, parts,
            pltpu.VMEM((8 * depth, count), jnp.bfloat16), pltpu.VMEM((count, 2 * LANES), jnp.bfloat16),
            pltpu.VMEM((2, dofs, dofs), jnp.float32), pltpu.VMEM((2 * dofs, 3 * dofs), jnp.bfloat16),
            dma((CHUNKS + 8,)), dma((2, CHUNKS + 1)), dma((2, CHUNKS + 1)), dma, dma((planes,)), dma, dma, dma,
            dma((2,)), dma((2,)), dma,
        ],
        compiler_params=pltpu.CompilerParams(collective_id=0, has_side_effects=True, vmem_limit_bytes=VMEM_LIMIT),
        name="exchange",
    )(field, edge_signs, face_nbrs, mu, eps, owner, trace_map, stiffness, mass)


def apply_kernel(
    received_ref, both_ref, squares_ref, size_ref, migrated_ref, applied_ref, out_ref
):
    @pl.when(pl.program_id(0) == 0)
    def _():
        out_ref[...] = jnp.sqrt(size_ref[...] * (squares_ref[...] / migrated_ref.shape[0]) + 1e-06)

    lane = lax.broadcasted_iota(jnp.int32, (8, LANES), 1)
    dofs = migrated_ref.shape[0]
    rows = dofs // 8
    both = both_ref[...]
    for t in range(0, received_ref.shape[0] // 4, 2):
        cols = slice(t * LANES, (t + 2) * LANES)
        found = [[], []]
        for h in range(2):
            for i in range(received_ref.shape[1] // 8):
                block = [received_ref[4 * (t + h) + q, 8 * i : 8 * i + 8, :] for q in range(4)]
                found[h].extend(quarter_swap(block, lane))
        value = jnp.concatenate([jnp.concatenate(part[:rows], axis=0) for part in found], axis=1)
        scale = jnp.concatenate([part[rows] for part in found], axis=1)
        migrated_ref[:, cols] = value
        product = stacked_product(both, value)
        applied_ref[:, cols] = scale[0:1] * product[:dofs] + scale[1:2] * product[dofs:]


def apply_received(received, both, squares, size):
    devices, depth, _ = received.shape
    dofs = both.shape[0] // 2
    per = 32
    block = per * 32
    return pl.pallas_call(
        apply_kernel,
        grid=(devices // per,),
        in_specs=[
            pl.BlockSpec((per, depth, LANES), lambda i: (i, 0, 0)),
            pl.BlockSpec(both.shape, lambda i: (0, 0)),
            pl.BlockSpec(squares.shape, lambda i: (0, 0)),
            pl.BlockSpec(squares.shape, lambda i: (0, 0)),
        ],
        out_specs=[pl.BlockSpec((dofs, block), lambda i: (0, i))] * 2 + [pl.BlockSpec(squares.shape, lambda i: (0, 0))],
        out_shape=[jax.ShapeDtypeStruct((dofs, devices * 32), jnp.float32)] * 2
        + [jax.ShapeDtypeStruct(squares.shape, jnp.float32)],
        compiler_params=pltpu.CompilerParams(vmem_limit_bytes=VMEM_LIMIT),
        cost_estimate=pl.CostEstimate(flops=10**9, bytes_accessed=8 * 10**6, transcendentals=0),
        name="apply",
    )(received, both, squares, size)


def body(field, edge_signs, face_nbrs, elem_size, mu_inv, permittivity, new_owner, trace_map, stiffness, mass):
    count = field.shape[1]
    devices = lax.axis_size(AXES)
    row = (1, count)
    squares, received, both = exchange(
        field, edge_signs, face_nbrs, mu_inv.reshape(row), permittivity.reshape(row), new_owner.reshape(row),
        trace_map, stiffness, mass, devices,
    )
    migrated, applied, indicators = apply_received(received, both, squares, elem_size.reshape(row))
    return indicators.reshape(count), migrated, applied


def solution(mesh):
    flat = P(AXES)
    wide = P(None, AXES)
    in_specs = (wide, wide, wide, flat, flat, flat, P(AXES, None), P(), P(), P())
    return jax.shard_map(body, mesh=mesh, in_specs=in_specs, out_specs=(flat, wide, wide), check_vma=False)
```

```python
import functools

import jax
import jax.numpy as jnp
from jax import lax
from jax.experimental import pallas as pl
from jax.experimental.pallas import tpu as pltpu
from jax.sharding import PartitionSpec as P

AXES = ("gx", "yz")
LANES = 128
VMEM_LIMIT = 60 << 20


def split3(value):
    high = value.astype(jnp.bfloat16)
    low = (value - high.astype(jnp.float32)).astype(jnp.bfloat16)
    return high, low


def stacked_left(matrix):
    high, low = split3(jnp.transpose(matrix))
    return jnp.concatenate([high, high, low], axis=1)


def stacked_product(left, right):
    high, low = split3(right)
    return jnp.dot(left, jnp.concatenate([high, low, high], axis=0), preferred_element_type=jnp.float32)


def lane_gather(table, index):
    return jnp.take_along_axis(table, index, axis=1)


def row8(row):
    return jnp.broadcast_to(row, (8, LANES))


def quarter_swap(parts, lane):
    upper = (lane & 64) != 0
    odd = (lane & 32) != 0
    a0, a1, a2, a3 = parts
    b0 = jnp.where(upper, pltpu.roll(a2, 64, 1), a0)
    b2 = jnp.where(upper, a2, pltpu.roll(a0, 64, 1))
    b1 = jnp.where(upper, pltpu.roll(a3, 64, 1), a1)
    b3 = jnp.where(upper, a3, pltpu.roll(a1, 64, 1))
    c0 = jnp.where(odd, pltpu.roll(b1, 32, 1), b0)
    c1 = jnp.where(odd, b1, pltpu.roll(b0, 96, 1))
    c2 = jnp.where(odd, pltpu.roll(b3, 32, 1), b2)
    c3 = jnp.where(odd, b3, pltpu.roll(b2, 96, 1))
    return c0, c1, c2, c3


MESH = pl.DeviceIdType.MESH
CHUNKS = 4
MATRIX_FACES = (0, 1, 3, 5)


def bit(k, n):
    return lax.rem(lax.div(k, 2**n), 2)


def offsets(k):
    return bit(k, 1) + 2 * bit(k, 3), bit(k, 4), bit(k, 0) + 2 * bit(k, 2)


def exchange_kernel(
    field_ref, signs_ref, nbrs_ref, mu_ref, eps_ref, owner_ref, map_ref, stiffness_ref, mass_ref,
    squares_ref, received_ref, both_ref,
    oriented, traces, halo_traces, halo_nbrs, signs, nbrs, mu, eps, owner, tmap, scale, high_ref, low_ref, payload, bundle,
    reply_out, reply_in, own_parts, halo_parts, columns, picks_ref, matrices, both,
    in_sem, halo_send, halo_recv, a_send, a_recv, f_send, f_recv, own_sem, reply_send, reply_recv, both_sem,
):
    gx = lax.axis_index("gx")
    yz = lax.axis_index("yz")
    gx_size = lax.axis_size("gx")
    yz_size = lax.axis_size("yz")
    devices = gx_size * yz_size
    me = gx * yz_size + yz
    z, c = lax.div(gx, 2), lax.rem(gx, 2)
    y, x = lax.div(yz, 4), lax.rem(yz, 4)
    plane = gx * 4 + y
    planes = devices // 4
    dofs, count = oriented.shape
    depth = payload.shape[1]
    block = count // CHUNKS

    def at(index):
        return (lax.div(index, yz_size), lax.rem(index, yz_size))

    def in_plane(p):
        return (lax.div(p, 4), lax.rem(p, 4) * 4 + x)

    def target(k):
        oz, oc, oy = offsets(k)
        return (lax.rem(z + oz, 4) * 2 + lax.rem(c + oc, 2)) * 4 + lax.rem(y + oy, 4)

    def source(k):
        oz, oc, oy = offsets(k)
        return (lax.rem(z + 4 - oz, 4) * 2 + lax.rem(c + 2 - oc, 2)) * 4 + lax.rem(y + 4 - oy, 4)

    following = lax.rem(me + 1, devices)
    preceding = lax.rem(me + devices - 1, devices)
    ahead, behind = at(following), at(preceding)
    up_index = jnp.where(c == 0, preceding, following)
    down_index = jnp.where(c == 0, following, preceding)
    up, down = at(up_index), at(down_index)
    sink = (c == 1) & (yz == 0)
    source_end = (c == 0) & (yz == 0)
    halo_count = jnp.where(sink, 2, jnp.where(source_end, 0, 1))
    landing_slot = jnp.where((c == 0) & (yz == yz_size - 1), 1, 0)
    reply_slot = jnp.where((c == 1) & (yz == yz_size - 1), 1, 0)

    loads = [
        pltpu.make_async_copy(signs_ref, signs, in_sem.at[0]),
        pltpu.make_async_copy(map_ref, tmap, in_sem.at[1]),
    ]
    fields = []
    for part in range(CHUNKS):
        cols = pl.ds(part * block, block)
        fields.append(pltpu.make_async_copy(field_ref.at[:, cols], oriented.at[:, cols], in_sem.at[2 + part]))
    later = [
        pltpu.make_async_copy(s, d, in_sem.at[2 + CHUNKS + i])
        for i, (s, d) in enumerate(
            (
                (owner_ref, owner), (mu_ref, mu), (eps_ref, eps), (nbrs_ref, nbrs),
                (stiffness_ref, matrices.at[0]), (mass_ref, matrices.at[1]),
            )
        )
    ]
    for copy in loads + fields + later:
        copy.start()

    barrier = pltpu.get_barrier_semaphore()

    def greet(k, carry):
        pl.semaphore_signal(barrier, inc=1, device_id=in_plane(target(k)), device_id_type=MESH)
        return carry

    lax.fori_loop(1, planes, greet, 0)
    for step in range(1, 4):
        pl.semaphore_signal(barrier, inc=1, device_id=(gx, y * 4 + lax.rem(x + step, 4)), device_id_type=MESH)
    pl.semaphore_signal(barrier, inc=1, device_id=ahead, device_id_type=MESH)
    pl.semaphore_signal(barrier, inc=1, device_id=behind, device_id_type=MESH)

    edges = signs.shape[0]
    rows = lax.broadcasted_iota(jnp.int32, (40, edges), 0)
    edge = lax.broadcasted_iota(jnp.int32, (40, edges), 1)
    picks = ((rows < 36) & (rows % 3 != 1) & (rows // 3 == edge)).astype(jnp.bfloat16)

    def halo_copy(part, lane_of, slot, peer):
        cols = pl.ds(part * block, block)
        if part == CHUNKS:
            src, dst = nbrs, halo_nbrs.at[slot]
        else:
            src, dst = traces.at[:, cols], halo_traces.at[slot, :, cols]
        return pltpu.make_async_remote_copy(
            src_ref=src, dst_ref=dst, send_sem=halo_send.at[lane_of, part], recv_sem=halo_recv.at[slot, part],
            device_id=peer, device_id_type=MESH,
        )

    def halo_start(part):
        @pl.when(jnp.logical_not(sink))
        def _():
            halo_copy(part, 0, landing_slot, down).start()

        @pl.when(source_end)
        def _():
            halo_copy(part, 1, 0, up).start()

    for copy in loads:
        copy.wait()
    map_parts = stacked_left(tmap[...])
    for part in range(CHUNKS):
        cols = slice(part * block, (part + 1) * block)
        fields[part].wait()
        shifted = (signs[:, cols] - 1).astype(jnp.float32).astype(jnp.bfloat16)
        factor = 1.0 + jnp.dot(picks, shifted, preferred_element_type=jnp.float32)
        oriented[0:40, cols] = oriented[0:40, cols] * factor
        traces[:, cols] = stacked_product(map_parts, oriented[:, cols])
        if part == 1:
            pl.semaphore_wait(barrier, planes - 1 + 3 + 2)
        if part >= 1:
            halo_start(part - 1)
    for copy in later:
        copy.wait()
    halo_start(CHUNKS)

    tiles = count // LANES
    bf = jnp.bfloat16
    sub = lax.broadcasted_iota(jnp.int32, (LANES, LANES), 0)
    lane_full = lax.broadcasted_iota(jnp.int32, (LANES, LANES), 1)
    upto = (sub <= lane_full).astype(jnp.float32).astype(bf)
    ones = jnp.ones((LANES, LANES), bf)
    before = jnp.zeros((LANES, LANES), jnp.float32)
    nt = (((1,), (1,)), ((), ()))
    table = jnp.zeros((3 * planes, LANES), jnp.float32)
    sub8 = lax.broadcasted_iota(jnp.int32, (8, LANES), 0)
    for tile in range(tiles):
        cols = slice(tile * LANES, (tile + 1) * LANES)
        scale[:, cols] = jnp.where(sub8 == 0, row8(mu[:, cols]), jnp.where(sub8 == 1, row8(eps[:, cols]), 0.0))
        own = owner[:, cols]
        onehot = sub == own
        hot = onehot.astype(jnp.float32)
        hot16 = hot.astype(bf)
        ordinal = before + jnp.dot(hot16, upto, preferred_element_type=jnp.float32) - 1.0
        rank = jnp.sum(jnp.where(onehot, ordinal, 0.0), axis=0, keepdims=True)
        before = before + jnp.dot(hot16, ones, preferred_element_type=jnp.float32)
        place = (own & 3) * 32 + rank.astype(jnp.int32)
        landing = (sub == place).astype(jnp.float32).astype(bf)
        group = lax.broadcasted_iota(jnp.int32, (planes, LANES), 0) == (own >> 2)
        groupf = group.astype(jnp.float32)
        lane_row = lax.broadcasted_iota(jnp.int32, (planes, LANES), 1).astype(jnp.float32)
        parts = jnp.concatenate([groupf, groupf * lane_row, groupf * float(tile)], axis=0).astype(bf)
        table = table + lax.dot_general(parts, landing, nt, preferred_element_type=jnp.float32)
    found = table[:planes]
    high_ref[...] = jnp.where(found > 0.5, table[2 * planes :], -1.0).astype(jnp.int32)
    low_ref[...] = table[planes : 2 * planes].astype(jnp.int32)
    halo_start(CHUNKS - 1)

    lane = lax.broadcasted_iota(jnp.int32, (8, LANES), 1)
    pair = 2 * LANES
    sub_pair = lax.broadcasted_iota(jnp.int32, (LANES, pair), 0)
    groups = -(-depth // 8)
    tail = depth - 8 * (groups - 1)
    height = 32 * groups
    main = 32 * (groups - 1)
    spot_row = lax.broadcasted_iota(jnp.int32, (32, dofs - main + 8), 0)
    item = lax.broadcasted_iota(jnp.int32, (32, dofs - main + 8), 1)
    inner = lax.rem(spot_row, 8)
    places = ((inner < tail) & (item == lax.div(spot_row, 8) * tail + inner)).astype(jnp.float32).astype(bf)
    for part in range(CHUNKS):
        cols = slice(part * block, (part + 1) * block)
        columns[0:main, cols], columns[height : height + main, cols] = split3(oriented[0:main, cols])
        rest_parts = split3(jnp.concatenate([oriented[main:, cols], scale[:, cols]], axis=0))
        for i, piece in enumerate(rest_parts):
            moved_rows = jnp.dot(places, piece, preferred_element_type=jnp.float32).astype(bf)
            columns[height * i + main : height * (i + 1), cols] = moved_rows

    def pack_pair(k):
        two = (target(k), target(k + 1))
        high = jnp.concatenate([high_ref[pl.ds(t, 1), :] for t in two], axis=1)
        low = jnp.concatenate([low_ref[pl.ds(t, 1), :] for t in two], axis=1)
        pick = (sub_pair == low).astype(jnp.float32).astype(bf)
        for tile in range(tiles):
            gate = jnp.broadcast_to((high == tile).astype(jnp.float32), (16, pair)).astype(bf)
            picks_ref[tile * LANES : (tile + 1) * LANES, :] = pick * jnp.concatenate([gate] * 8, axis=0)
        found = jnp.dot(columns[...], picks_ref[...], preferred_element_type=jnp.float32)
        value = found[:height] + found[height:]
        for h, t in enumerate(two):
            lanes = slice(h * LANES, (h + 1) * LANES)
            for i in range(groups):
                outs = quarter_swap([value[32 * i + 8 * q : 32 * i + 8 * q + 8, lanes] for q in range(4)], lane)
                kept = 8 if i < groups - 1 else tail
                for q in range(4):
                    payload[4 * t + q, 8 * i : 8 * i + kept, :] = outs[q][:kept]

    def send_group(k):
        t = target(k)
        pltpu.make_async_remote_copy(
            src_ref=payload.at[pl.ds(4 * t, 4)], dst_ref=bundle.at[pl.ds(4 * plane, 4)], send_sem=a_send,
            recv_sem=a_recv.at[plane], device_id=in_plane(t), device_id_type=MESH,
        ).start()

    def forward(origin, s):
        for step in range(1, 4):
            xd = lax.rem(x + step, 4)
            pltpu.make_async_remote_copy(
                src_ref=origin.at[4 * s + xd], dst_ref=received_ref.at[4 * s + x], send_sem=f_send, recv_sem=f_recv,
                device_id=(gx, y * 4 + xd), device_id_type=MESH,
            ).start()
        pltpu.make_async_copy(origin.at[4 * s + x], received_ref.at[4 * s + x], own_sem).start()

    def forward_step(k):
        s = source(k)
        pltpu.make_async_remote_copy(
            src_ref=payload.at[pl.ds(4 * s, 4)], dst_ref=bundle.at[pl.ds(4 * s, 4)], send_sem=a_send,
            recv_sem=a_recv.at[s], device_id=ahead, device_id_type=MESH,
        ).wait_recv()
        forward(bundle, s)

    lag = 6

    def pack_step(m, carry):
        pack_pair(2 * m)

        @pl.when(m == 1)
        def _():
            forward(payload, plane)

        @pl.when(m > 1)
        def _():
            send_group(2 * m - 2)

        @pl.when(m > 0)
        def _():
            send_group(2 * m - 1)

        @pl.when(m >= lag)
        def _():
            forward_step(m - lag + 1)

        return carry

    lax.fori_loop(0, planes // 2, pack_step, 0)
    send_group(planes - 2)
    send_group(planes - 1)
    done = planes // 2 - lag + 1

    width = dofs // 6
    vecs = width // 8

    def split_table(table, out):
        for o, odd in enumerate(MATRIX_FACES):
            rows_o = slice(odd * width, (odd + 1) * width)
            for tile in range(0, tiles, 2):
                stacked = jnp.concatenate(
                    [table[rows_o, (tile + i) * LANES : (tile + i + 1) * LANES] for i in range(2)], axis=0
                )
                high, low = split3(stacked)
                out[o, tile * width : (tile + 2) * width, 0:LANES] = high
                out[o, tile * width : (tile + 2) * width, LANES:] = low

    def jump_tile(step, faces, face_nbrs, table, parts, base, alone):
        cols = pl.ds(pl.multiple_of(step * pair, pair), pair)
        total = jnp.zeros((8, pair), jnp.float32)
        for face in range(6):
            other = face ^ 1
            nbr = jnp.broadcast_to(face_nbrs[face : face + 1, cols], (8, pair))
            spot = nbr - base
            high = spot >> 7
            low = spot & (LANES - 1)
            if other in MATRIX_FACES:
                pick = (sub_pair == low[0:1]).astype(jnp.float32).astype(jnp.bfloat16)
                found = jnp.dot(
                    parts[MATRIX_FACES.index(other)], jnp.concatenate([pick, pick], axis=0), preferred_element_type=jnp.float32
                )
                got = [jnp.zeros((8, pair), jnp.float32) for _ in range(vecs)]
                for tile in range(tiles):
                    hit = high == tile
                    for v in range(vecs):
                        r = tile * width + 8 * v
                        got[v] = jnp.where(hit, found[r : r + 8], got[v])
            else:
                halves = []
                for h in range(2):
                    lanes = slice(h * LANES, (h + 1) * LANES)
                    half = [jnp.zeros((8, LANES), jnp.float32) for _ in range(vecs)]
                    for tile in range(tiles):
                        hit = high[:, lanes] == tile
                        for v in range(vecs):
                            r = other * width + 8 * v
                            piece = table[r : r + 8, tile * LANES : (tile + 1) * LANES]
                            half[v] = jnp.where(hit, lane_gather(piece, low[:, lanes]), half[v])
                    halves.append(half)
                got = [jnp.concatenate([halves[0][v], halves[1][v]], axis=1) for v in range(vecs)]
            here = (spot >= 0) & (spot < count)
            if alone:
                here = here | (nbr < 0)
            for v in range(vecs):
                r = face * width + 8 * v
                jump = faces[r : r + 8, cols] - got[v]
                total = total + jnp.where(here, jump * jump, 0.0)
        return cols, jnp.sum(total, axis=0, keepdims=True)

    own_base = me * count

    for i in range(2):
        both[dofs * i : dofs * (i + 1)] = stacked_left(matrices[i])
    hand_over = pltpu.make_async_copy(both, both_ref, both_sem)
    split_table(traces, own_parts)

    hand_over.start()

    def own_step(step, carry):
        forward_step(done + step)
        cols, row = jump_tile(step, traces, nbrs, traces, own_parts, own_base, True)
        squares_ref[:, cols] = row
        return carry

    lax.fori_loop(0, tiles // 2, own_step, 0)
    rest = done + tiles // 2

    def halo_step(i, carry):
        for part in range(CHUNKS + 1):
            halo_copy(part, 0, i, up).wait_recv()
        base = jnp.where(i == 0, up_index, down_index) * count
        split_table(halo_traces.at[i], halo_parts)

        def across(step, inner):
            first = rest + jnp.where(sink, i * (tiles // 2) + step, 2 * step)
            second = rest + 2 * step + 1

            @pl.when(first < planes)
            def _():
                forward_step(first)

            @pl.when(jnp.logical_not(sink) & (second < planes))
            def _():
                forward_step(second)

            cols, row = jump_tile(step, traces, nbrs, halo_traces.at[i], halo_parts, base, False)
            squares_ref[:, cols] = squares_ref[:, cols] + row
            cols, row = jump_tile(step, halo_traces.at[i], halo_nbrs.at[i], traces, own_parts, own_base, False)
            reply_out[i, :, cols] = row
            return inner

        lax.fori_loop(0, tiles // 2, across, 0)
        return carry

    lax.fori_loop(0, halo_count, halo_step, 0)

    @pl.when(source_end)
    def _():
        def remaining(k, carry):
            forward_step(k)
            return carry

        lax.fori_loop(rest, planes, remaining, 0)

    def reply(slot, landing, peer):
        return pltpu.make_async_remote_copy(
            src_ref=reply_out.at[slot], dst_ref=reply_in.at[landing], send_sem=reply_send.at[slot],
            recv_sem=reply_recv.at[landing], device_id=peer, device_id_type=MESH,
        )

    @pl.when(jnp.logical_not(source_end))
    def _():
        reply(0, reply_slot, up).start()

    @pl.when(sink)
    def _():
        reply(1, 0, down).start()

    @pl.when(jnp.logical_not(sink))
    def _():
        reply(0, 0, up).wait_recv()
        squares_ref[...] = squares_ref[...] + reply_in[0]

    @pl.when(source_end)
    def _():
        reply(0, 1, up).wait_recv()
        squares_ref[...] = squares_ref[...] + reply_in[1]

    hand_over.wait()
    @pl.when(jnp.logical_not(source_end))
    def _():
        reply(0, reply_slot, up).wait_send()

    @pl.when(sink)
    def _():
        reply(1, 0, down).wait_send()

    for part in range(CHUNKS + 1):

        @pl.when(jnp.logical_not(sink))
        def _():
            halo_copy(part, 0, landing_slot, down).wait_send()

        @pl.when(source_end)
        def _():
            halo_copy(part, 1, 0, up).wait_send()

    sent = 4 * (planes - 1)
    pltpu.make_async_remote_copy(
        src_ref=payload.at[pl.ds(0, sent)], dst_ref=bundle.at[pl.ds(0, sent)], send_sem=a_send, recv_sem=a_recv.at[0],
        device_id=ahead, device_id_type=MESH,
    ).wait_send()
    moved = 3 * planes
    along = pltpu.make_async_remote_copy(
        src_ref=bundle.at[pl.ds(0, moved)], dst_ref=received_ref.at[pl.ds(0, moved)], send_sem=f_send, recv_sem=f_recv,
        device_id=ahead, device_id_type=MESH,
    )
    along.wait_send()
    along.wait_recv()
    pltpu.make_async_copy(bundle.at[pl.ds(0, planes)], received_ref.at[pl.ds(0, planes)], own_sem).wait()


def exchange(field, edge_signs, face_nbrs, mu, eps, owner, trace_map, stiffness, mass, devices):
    dofs, count = field.shape
    planes = devices // 4
    depth = -(-(dofs + 2) // 4)
    anywhere = pl.BlockSpec(memory_space=pl.ANY)
    wide = pltpu.VMEM((dofs, count), jnp.float32)
    blocks = pltpu.VMEM((devices, depth, LANES), jnp.float32)
    row = pltpu.VMEM((1, count), jnp.float32)
    parts = pltpu.VMEM((len(MATRIX_FACES), count // LANES * dofs // 6, 2 * LANES), jnp.bfloat16)
    dma = pltpu.SemaphoreType.DMA
    return pl.pallas_call(
        exchange_kernel,
        in_specs=[anywhere] * 9,
        out_specs=[pl.BlockSpec(memory_space=pltpu.VMEM), anywhere, anywhere],
        out_shape=[
            jax.ShapeDtypeStruct((1, count), jnp.float32),
            jax.ShapeDtypeStruct((devices, depth, LANES), jnp.float32),
            jax.ShapeDtypeStruct((2 * dofs, 3 * dofs), jnp.bfloat16),
        ],
        scratch_shapes=[
            wide, wide, pltpu.VMEM((2, dofs, count), jnp.float32), pltpu.VMEM((2, *face_nbrs.shape), jnp.int32),
            pltpu.VMEM(edge_signs.shape, jnp.int32),
            pltpu.VMEM(face_nbrs.shape, jnp.int32),
            row, row, pltpu.VMEM((1, count), jnp.int32),
            pltpu.VMEM(trace_map.shape, jnp.float32),
            pltpu.VMEM((8, count), jnp.float32),
            pltpu.VMEM((planes, LANES), jnp.int32),
            pltpu.VMEM((planes, LANES), jnp.int32),
            blocks, blocks,
            pltpu.VMEM((2, 1, count), jnp.float32), pltpu.VMEM((2, 1, count), jnp.float32), parts, parts,
            pltpu.VMEM((64 * -(-depth // 8), count), jnp.bfloat16), pltpu.VMEM((count, 2 * LANES), jnp.bfloat16),
            pltpu.VMEM((2, dofs, dofs), jnp.float32), pltpu.VMEM((2 * dofs, 3 * dofs), jnp.bfloat16),
            dma((CHUNKS + 8,)), dma((2, CHUNKS + 1)), dma((2, CHUNKS + 1)), dma, dma((planes,)), dma, dma, dma,
            dma((2,)), dma((2,)), dma,
        ],
        compiler_params=pltpu.CompilerParams(collective_id=0, has_side_effects=True, vmem_limit_bytes=VMEM_LIMIT),
        name="exchange",
    )(field, edge_signs, face_nbrs, mu, eps, owner, trace_map, stiffness, mass)


def apply_kernel(
    received_ref, both_ref, squares_ref, size_ref, migrated_ref, applied_ref, out_ref
):
    @pl.when(pl.program_id(0) == 0)
    def _():
        out_ref[...] = jnp.sqrt(size_ref[...] * (squares_ref[...] / migrated_ref.shape[0]) + 1e-06)

    lane = lax.broadcasted_iota(jnp.int32, (8, LANES), 1)
    dofs = migrated_ref.shape[0]
    groups = -(-received_ref.shape[1] // 8)
    tail = received_ref.shape[1] - 8 * (groups - 1)
    both = both_ref[...]
    for t in range(0, received_ref.shape[0] // 4, 2):
        cols = slice(t * LANES, (t + 2) * LANES)
        found = [[], []]
        for h in range(2):
            for i in range(groups):
                kept = 8 if i < groups - 1 else tail
                block = [received_ref[4 * (t + h) + q, 8 * i : 8 * i + kept, :] for q in range(4)]
                if kept < 8:
                    block = [jnp.concatenate([b, jnp.zeros((8 - kept, LANES), jnp.float32)], axis=0) for b in block]
                found[h].extend(piece[:kept] for piece in quarter_swap(block, lane))
        stacked = [jnp.concatenate(part, axis=0) for part in found]
        value = jnp.concatenate([part[:dofs] for part in stacked], axis=1)
        scale = jnp.concatenate([part[dofs : dofs + 2] for part in stacked], axis=1)
        migrated_ref[:, cols] = value
        product = stacked_product(both, value)
        applied_ref[:, cols] = scale[0:1] * product[:dofs] + scale[1:2] * product[dofs:]


def apply_received(received, both, squares, size):
    devices, depth, _ = received.shape
    dofs = both.shape[0] // 2
    per = 32
    block = per * 32
    return pl.pallas_call(
        apply_kernel,
        grid=(devices // per,),
        in_specs=[
            pl.BlockSpec((per, depth, LANES), lambda i: (i, 0, 0)),
            pl.BlockSpec(both.shape, lambda i: (0, 0)),
            pl.BlockSpec(squares.shape, lambda i: (0, 0)),
            pl.BlockSpec(squares.shape, lambda i: (0, 0)),
        ],
        out_specs=[pl.BlockSpec((dofs, block), lambda i: (0, i))] * 2 + [pl.BlockSpec(squares.shape, lambda i: (0, 0))],
        out_shape=[jax.ShapeDtypeStruct((dofs, devices * 32), jnp.float32)] * 2
        + [jax.ShapeDtypeStruct(squares.shape, jnp.float32)],
        compiler_params=pltpu.CompilerParams(vmem_limit_bytes=VMEM_LIMIT),
        cost_estimate=pl.CostEstimate(flops=10**9, bytes_accessed=8 * 10**6, transcendentals=0),
        name="apply",
    )(received, both, squares, size)


def body(field, edge_signs, face_nbrs, elem_size, mu_inv, permittivity, new_owner, trace_map, stiffness, mass):
    count = field.shape[1]
    devices = lax.axis_size(AXES)
    row = (1, count)
    squares, received, both = exchange(
        field, edge_signs, face_nbrs, mu_inv.reshape(row), permittivity.reshape(row), new_owner.reshape(row),
        trace_map, stiffness, mass, devices,
    )
    migrated, applied, indicators = apply_received(received, both, squares, elem_size.reshape(row))
    return indicators.reshape(count), migrated, applied


def solution(mesh):
    flat = P(AXES)
    wide = P(None, AXES)
    in_specs = (wide, wide, wide, flat, flat, flat, P(AXES, None), P(), P(), P())
    return jax.shard_map(body, mesh=mesh, in_specs=in_specs, out_specs=(flat, wide, wide), check_vma=False)
```

```python
import functools

import jax
import jax.numpy as jnp
from jax import lax
from jax.experimental import pallas as pl
from jax.experimental.pallas import tpu as pltpu
from jax.sharding import PartitionSpec as P

AXES = ("gx", "yz")
LANES = 128
VMEM_LIMIT = 60 << 20


def split3(value):
    high = value.astype(jnp.bfloat16)
    low = (value - high.astype(jnp.float32)).astype(jnp.bfloat16)
    return high, low


def stacked_left(matrix):
    high, low = split3(jnp.transpose(matrix))
    return jnp.concatenate([high, high, low], axis=1)


def stacked_product(left, right):
    high, low = split3(right)
    return jnp.dot(left, jnp.concatenate([high, low, high], axis=0), preferred_element_type=jnp.float32)


def lane_gather(table, index):
    return jnp.take_along_axis(table, index, axis=1)


def row8(row):
    return jnp.broadcast_to(row, (8, LANES))


def quarter_swap(parts, lane):
    upper = (lane & 64) != 0
    odd = (lane & 32) != 0
    a0, a1, a2, a3 = parts
    b0 = jnp.where(upper, pltpu.roll(a2, 64, 1), a0)
    b2 = jnp.where(upper, a2, pltpu.roll(a0, 64, 1))
    b1 = jnp.where(upper, pltpu.roll(a3, 64, 1), a1)
    b3 = jnp.where(upper, a3, pltpu.roll(a1, 64, 1))
    c0 = jnp.where(odd, pltpu.roll(b1, 32, 1), b0)
    c1 = jnp.where(odd, b1, pltpu.roll(b0, 96, 1))
    c2 = jnp.where(odd, pltpu.roll(b3, 32, 1), b2)
    c3 = jnp.where(odd, b3, pltpu.roll(b2, 96, 1))
    return c0, c1, c2, c3


MESH = pl.DeviceIdType.MESH
CHUNKS = 4
MATRIX_FACES = (0, 1, 3, 5)


def bit(k, n):
    return lax.rem(lax.div(k, 2**n), 2)


def offsets(k):
    return bit(k, 2) + 2 * bit(k, 3), bit(k, 4), bit(k, 0) + 2 * bit(k, 1)


def exchange_kernel(
    field_ref, signs_ref, nbrs_ref, mu_ref, eps_ref, owner_ref, map_ref, stiffness_ref, mass_ref,
    squares_ref, received_ref, both_ref,
    oriented, traces, halo_traces, halo_nbrs, signs, nbrs, mu, eps, owner, tmap, scale, high_ref, low_ref, payload, bundle,
    reply_out, reply_in, own_parts, halo_parts, columns, picks_ref, matrices, both,
    in_sem, halo_send, halo_recv, a_send, a_recv, f_send, f_recv, own_sem, reply_send, reply_recv, both_sem,
):
    gx = lax.axis_index("gx")
    yz = lax.axis_index("yz")
    gx_size = lax.axis_size("gx")
    yz_size = lax.axis_size("yz")
    devices = gx_size * yz_size
    me = gx * yz_size + yz
    z, c = lax.div(gx, 2), lax.rem(gx, 2)
    y, x = lax.div(yz, 4), lax.rem(yz, 4)
    plane = gx * 4 + y
    planes = devices // 4
    dofs, count = oriented.shape
    depth = payload.shape[1]
    block = count // CHUNKS

    def at(index):
        return (lax.div(index, yz_size), lax.rem(index, yz_size))

    def in_plane(p):
        return (lax.div(p, 4), lax.rem(p, 4) * 4 + x)

    def target(k):
        oz, oc, oy = offsets(k)
        return (lax.rem(z + oz, 4) * 2 + lax.rem(c + oc, 2)) * 4 + lax.rem(y + oy, 4)

    def source(k):
        oz, oc, oy = offsets(k)
        return (lax.rem(z + 4 - oz, 4) * 2 + lax.rem(c + 2 - oc, 2)) * 4 + lax.rem(y + 4 - oy, 4)

    following = lax.rem(me + 1, devices)
    preceding = lax.rem(me + devices - 1, devices)
    ahead, behind = at(following), at(preceding)
    up_index = jnp.where(c == 0, preceding, following)
    down_index = jnp.where(c == 0, following, preceding)
    up, down = at(up_index), at(down_index)
    sink = (c == 1) & (yz == 0)
    source_end = (c == 0) & (yz == 0)
    halo_count = jnp.where(sink, 2, jnp.where(source_end, 0, 1))
    landing_slot = jnp.where((c == 0) & (yz == yz_size - 1), 1, 0)
    reply_slot = jnp.where((c == 1) & (yz == yz_size - 1), 1, 0)

    loads = [
        pltpu.make_async_copy(signs_ref, signs, in_sem.at[0]),
        pltpu.make_async_copy(map_ref, tmap, in_sem.at[1]),
    ]
    fields = []
    for part in range(CHUNKS):
        cols = pl.ds(part * block, block)
        fields.append(pltpu.make_async_copy(field_ref.at[:, cols], oriented.at[:, cols], in_sem.at[2 + part]))
    later = [
        pltpu.make_async_copy(s, d, in_sem.at[2 + CHUNKS + i])
        for i, (s, d) in enumerate(
            (
                (owner_ref, owner), (mu_ref, mu), (eps_ref, eps), (nbrs_ref, nbrs),
                (stiffness_ref, matrices.at[0]), (mass_ref, matrices.at[1]),
            )
        )
    ]
    for copy in loads + fields + later:
        copy.start()

    barrier = pltpu.get_barrier_semaphore()

    def greet(k, carry):
        pl.semaphore_signal(barrier, inc=1, device_id=in_plane(target(k)), device_id_type=MESH)
        return carry

    lax.fori_loop(1, planes, greet, 0)
    for step in range(1, 4):
        pl.semaphore_signal(barrier, inc=1, device_id=(gx, y * 4 + lax.rem(x + step, 4)), device_id_type=MESH)
    pl.semaphore_signal(barrier, inc=1, device_id=ahead, device_id_type=MESH)
    pl.semaphore_signal(barrier, inc=1, device_id=behind, device_id_type=MESH)

    edges = signs.shape[0]
    rows = lax.broadcasted_iota(jnp.int32, (40, edges), 0)
    edge = lax.broadcasted_iota(jnp.int32, (40, edges), 1)
    picks = ((rows < 36) & (rows % 3 != 1) & (rows // 3 == edge)).astype(jnp.bfloat16)

    def halo_copy(part, lane_of, slot, peer):
        cols = pl.ds(part * block, block)
        if part == CHUNKS:
            src, dst = nbrs, halo_nbrs.at[slot]
        else:
            src, dst = traces.at[:, cols], halo_traces.at[slot, :, cols]
        return pltpu.make_async_remote_copy(
            src_ref=src, dst_ref=dst, send_sem=halo_send.at[lane_of, part], recv_sem=halo_recv.at[slot, part],
            device_id=peer, device_id_type=MESH,
        )

    def halo_start(part):
        @pl.when(jnp.logical_not(sink))
        def _():
            halo_copy(part, 0, landing_slot, down).start()

        @pl.when(source_end)
        def _():
            halo_copy(part, 1, 0, up).start()

    for copy in loads:
        copy.wait()
    map_parts = stacked_left(tmap[...])
    for part in range(CHUNKS):
        cols = slice(part * block, (part + 1) * block)
        fields[part].wait()
        shifted = (signs[:, cols] - 1).astype(jnp.float32).astype(jnp.bfloat16)
        factor = 1.0 + jnp.dot(picks, shifted, preferred_element_type=jnp.float32)
        oriented[0:40, cols] = oriented[0:40, cols] * factor
        traces[:, cols] = stacked_product(map_parts, oriented[:, cols])
        if part == 1:
            pl.semaphore_wait(barrier, planes - 1 + 3 + 2)
        if part >= 1:
            halo_start(part - 1)
    for copy in later:
        copy.wait()
    halo_start(CHUNKS)

    tiles = count // LANES
    bf = jnp.bfloat16
    sub = lax.broadcasted_iota(jnp.int32, (LANES, LANES), 0)
    lane_full = lax.broadcasted_iota(jnp.int32, (LANES, LANES), 1)
    upto = (sub <= lane_full).astype(jnp.float32).astype(bf)
    ones = jnp.ones((LANES, LANES), bf)
    before = jnp.zeros((LANES, LANES), jnp.float32)
    nt = (((1,), (1,)), ((), ()))
    table = jnp.zeros((3 * planes, LANES), jnp.float32)
    sub8 = lax.broadcasted_iota(jnp.int32, (8, LANES), 0)
    for tile in range(tiles):
        cols = slice(tile * LANES, (tile + 1) * LANES)
        scale[:, cols] = jnp.where(sub8 == 0, row8(mu[:, cols]), jnp.where(sub8 == 1, row8(eps[:, cols]), 0.0))
        own = owner[:, cols]
        onehot = sub == own
        hot = onehot.astype(jnp.float32)
        hot16 = hot.astype(bf)
        ordinal = before + jnp.dot(hot16, upto, preferred_element_type=jnp.float32) - 1.0
        rank = jnp.sum(jnp.where(onehot, ordinal, 0.0), axis=0, keepdims=True)
        before = before + jnp.dot(hot16, ones, preferred_element_type=jnp.float32)
        place = (own & 3) * 32 + rank.astype(jnp.int32)
        landing = (sub == place).astype(jnp.float32).astype(bf)
        group = lax.broadcasted_iota(jnp.int32, (planes, LANES), 0) == (own >> 2)
        groupf = group.astype(jnp.float32)
        lane_row = lax.broadcasted_iota(jnp.int32, (planes, LANES), 1).astype(jnp.float32)
        parts = jnp.concatenate([groupf, groupf * lane_row, groupf * float(tile)], axis=0).astype(bf)
        table = table + lax.dot_general(parts, landing, nt, preferred_element_type=jnp.float32)
    found = table[:planes]
    high_ref[...] = jnp.where(found > 0.5, table[2 * planes :], -1.0).astype(jnp.int32)
    low_ref[...] = table[planes : 2 * planes].astype(jnp.int32)
    halo_start(CHUNKS - 1)

    lane = lax.broadcasted_iota(jnp.int32, (8, LANES), 1)
    pair = 2 * LANES
    sub_pair = lax.broadcasted_iota(jnp.int32, (LANES, pair), 0)
    groups = -(-depth // 8)
    tail = depth - 8 * (groups - 1)
    height = 32 * groups
    main = 32 * (groups - 1)
    spot_row = lax.broadcasted_iota(jnp.int32, (32, dofs - main + 8), 0)
    item = lax.broadcasted_iota(jnp.int32, (32, dofs - main + 8), 1)
    inner = lax.rem(spot_row, 8)
    places = ((inner < tail) & (item == lax.div(spot_row, 8) * tail + inner)).astype(jnp.float32).astype(bf)
    for part in range(CHUNKS):
        cols = slice(part * block, (part + 1) * block)
        columns[0:main, cols], columns[height : height + main, cols] = split3(oriented[0:main, cols])
        rest_parts = split3(jnp.concatenate([oriented[main:, cols], scale[:, cols]], axis=0))
        for i, piece in enumerate(rest_parts):
            moved_rows = jnp.dot(places, piece, preferred_element_type=jnp.float32).astype(bf)
            columns[height * i + main : height * (i + 1), cols] = moved_rows

    def pack_pair(k):
        two = (target(k), target(k + 1))
        high = jnp.concatenate([high_ref[pl.ds(t, 1), :] for t in two], axis=1)
        low = jnp.concatenate([low_ref[pl.ds(t, 1), :] for t in two], axis=1)
        pick = (sub_pair == low).astype(jnp.float32).astype(bf)
        for tile in range(tiles):
            gate = jnp.broadcast_to((high == tile).astype(jnp.float32), (16, pair)).astype(bf)
            picks_ref[tile * LANES : (tile + 1) * LANES, :] = pick * jnp.concatenate([gate] * 8, axis=0)
        found = jnp.dot(columns[...], picks_ref[...], preferred_element_type=jnp.float32)
        value = found[:height] + found[height:]
        for h, t in enumerate(two):
            lanes = slice(h * LANES, (h + 1) * LANES)
            for i in range(groups):
                outs = quarter_swap([value[32 * i + 8 * q : 32 * i + 8 * q + 8, lanes] for q in range(4)], lane)
                kept = 8 if i < groups - 1 else tail
                for q in range(4):
                    payload[4 * t + q, 8 * i : 8 * i + kept, :] = outs[q][:kept]

    def send_group(k):
        t = target(k)
        pltpu.make_async_remote_copy(
            src_ref=payload.at[pl.ds(4 * t, 4)], dst_ref=bundle.at[pl.ds(4 * plane, 4)], send_sem=a_send,
            recv_sem=a_recv.at[plane], device_id=in_plane(t), device_id_type=MESH,
        ).start()

    def forward(origin, s):
        for step in range(1, 4):
            xd = lax.rem(x + step, 4)
            pltpu.make_async_remote_copy(
                src_ref=origin.at[4 * s + xd], dst_ref=received_ref.at[4 * s + x], send_sem=f_send, recv_sem=f_recv,
                device_id=(gx, y * 4 + xd), device_id_type=MESH,
            ).start()
        pltpu.make_async_copy(origin.at[4 * s + x], received_ref.at[4 * s + x], own_sem).start()

    def forward_step(k):
        s = source(k)
        pltpu.make_async_remote_copy(
            src_ref=payload.at[pl.ds(4 * s, 4)], dst_ref=bundle.at[pl.ds(4 * s, 4)], send_sem=a_send,
            recv_sem=a_recv.at[s], device_id=ahead, device_id_type=MESH,
        ).wait_recv()
        forward(bundle, s)

    lag = 8

    def pack_step(m, carry):
        pack_pair(2 * m)

        @pl.when(m == 1)
        def _():
            forward(payload, plane)

        @pl.when(m > 1)
        def _():
            send_group(2 * m - 2)

        @pl.when(m > 0)
        def _():
            send_group(2 * m - 1)

        @pl.when(m >= lag)
        def _():
            forward_step(m - lag + 1)

        return carry

    lax.fori_loop(0, planes // 2, pack_step, 0)
    send_group(planes - 2)
    send_group(planes - 1)
    done = planes // 2 - lag + 1

    width = dofs // 6
    vecs = width // 8

    def split_table(table, out):
        for o, odd in enumerate(MATRIX_FACES):
            rows_o = slice(odd * width, (odd + 1) * width)
            for tile in range(0, tiles, 2):
                stacked = jnp.concatenate(
                    [table[rows_o, (tile + i) * LANES : (tile + i + 1) * LANES] for i in range(2)], axis=0
                )
                high, low = split3(stacked)
                out[o, tile * width : (tile + 2) * width, 0:LANES] = high
                out[o, tile * width : (tile + 2) * width, LANES:] = low

    def jump_tile(step, faces, face_nbrs, table, parts, base, alone):
        cols = pl.ds(pl.multiple_of(step * pair, pair), pair)
        total = jnp.zeros((8, pair), jnp.float32)
        for face in range(6):
            other = face ^ 1
            nbr = jnp.broadcast_to(face_nbrs[face : face + 1, cols], (8, pair))
            spot = nbr - base
            high = spot >> 7
            low = spot & (LANES - 1)
            if other in MATRIX_FACES:
                pick = (sub_pair == low[0:1]).astype(jnp.float32).astype(jnp.bfloat16)
                found = jnp.dot(
                    parts[MATRIX_FACES.index(other)], jnp.concatenate([pick, pick], axis=0), preferred_element_type=jnp.float32
                )
                got = [jnp.zeros((8, pair), jnp.float32) for _ in range(vecs)]
                for tile in range(tiles):
                    hit = high == tile
                    for v in range(vecs):
                        r = tile * width + 8 * v
                        got[v] = jnp.where(hit, found[r : r + 8], got[v])
            else:
                halves = []
                for h in range(2):
                    lanes = slice(h * LANES, (h + 1) * LANES)
                    half = [jnp.zeros((8, LANES), jnp.float32) for _ in range(vecs)]
                    for tile in range(tiles):
                        hit = high[:, lanes] == tile
                        for v in range(vecs):
                            r = other * width + 8 * v
                            piece = table[r : r + 8, tile * LANES : (tile + 1) * LANES]
                            half[v] = jnp.where(hit, lane_gather(piece, low[:, lanes]), half[v])
                    halves.append(half)
                got = [jnp.concatenate([halves[0][v], halves[1][v]], axis=1) for v in range(vecs)]
            here = (spot >= 0) & (spot < count)
            if alone:
                here = here | (nbr < 0)
            for v in range(vecs):
                r = face * width + 8 * v
                jump = faces[r : r + 8, cols] - got[v]
                total = total + jnp.where(here, jump * jump, 0.0)
        return cols, jnp.sum(total, axis=0, keepdims=True)

    own_base = me * count

    for i in range(2):
        both[dofs * i : dofs * (i + 1)] = stacked_left(matrices[i])
    hand_over = pltpu.make_async_copy(both, both_ref, both_sem)
    split_table(traces, own_parts)

    hand_over.start()

    def own_step(step, carry):
        forward_step(done + step)
        cols, row = jump_tile(step, traces, nbrs, traces, own_parts, own_base, True)
        squares_ref[:, cols] = row
        return carry

    lax.fori_loop(0, tiles // 2, own_step, 0)
    rest = done + tiles // 2

    def halo_step(i, carry):
        for part in range(CHUNKS + 1):
            halo_copy(part, 0, i, up).wait_recv()
        base = jnp.where(i == 0, up_index, down_index) * count
        split_table(halo_traces.at[i], halo_parts)

        def across(step, inner):
            first = rest + jnp.where(sink, i * (tiles // 2) + step, 2 * step)
            second = rest + 2 * step + 1

            @pl.when(first < planes)
            def _():
                forward_step(first)

            @pl.when(jnp.logical_not(sink) & (second < planes))
            def _():
                forward_step(second)

            cols, row = jump_tile(step, traces, nbrs, halo_traces.at[i], halo_parts, base, False)
            squares_ref[:, cols] = squares_ref[:, cols] + row
            cols, row = jump_tile(step, halo_traces.at[i], halo_nbrs.at[i], traces, own_parts, own_base, False)
            reply_out[i, :, cols] = row
            return inner

        lax.fori_loop(0, tiles // 2, across, 0)
        return carry

    lax.fori_loop(0, halo_count, halo_step, 0)

    @pl.when(source_end)
    def _():
        def remaining(k, carry):
            forward_step(k)
            return carry

        lax.fori_loop(rest, planes, remaining, 0)

    def reply(slot, landing, peer):
        return pltpu.make_async_remote_copy(
            src_ref=reply_out.at[slot], dst_ref=reply_in.at[landing], send_sem=reply_send.at[slot],
            recv_sem=reply_recv.at[landing], device_id=peer, device_id_type=MESH,
        )

    @pl.when(jnp.logical_not(source_end))
    def _():
        reply(0, reply_slot, up).start()

    @pl.when(sink)
    def _():
        reply(1, 0, down).start()

    @pl.when(jnp.logical_not(sink))
    def _():
        reply(0, 0, up).wait_recv()
        squares_ref[...] = squares_ref[...] + reply_in[0]

    @pl.when(source_end)
    def _():
        reply(0, 1, up).wait_recv()
        squares_ref[...] = squares_ref[...] + reply_in[1]

    hand_over.wait()
    @pl.when(jnp.logical_not(source_end))
    def _():
        reply(0, reply_slot, up).wait_send()

    @pl.when(sink)
    def _():
        reply(1, 0, down).wait_send()

    for part in range(CHUNKS + 1):

        @pl.when(jnp.logical_not(sink))
        def _():
            halo_copy(part, 0, landing_slot, down).wait_send()

        @pl.when(source_end)
        def _():
            halo_copy(part, 1, 0, up).wait_send()

    sent = 4 * (planes - 1)
    pltpu.make_async_remote_copy(
        src_ref=payload.at[pl.ds(0, sent)], dst_ref=bundle.at[pl.ds(0, sent)], send_sem=a_send, recv_sem=a_recv.at[0],
        device_id=ahead, device_id_type=MESH,
    ).wait_send()
    moved = 3 * planes
    along = pltpu.make_async_remote_copy(
        src_ref=bundle.at[pl.ds(0, moved)], dst_ref=received_ref.at[pl.ds(0, moved)], send_sem=f_send, recv_sem=f_recv,
        device_id=ahead, device_id_type=MESH,
    )
    along.wait_send()
    along.wait_recv()
    pltpu.make_async_copy(bundle.at[pl.ds(0, planes)], received_ref.at[pl.ds(0, planes)], own_sem).wait()


def exchange(field, edge_signs, face_nbrs, mu, eps, owner, trace_map, stiffness, mass, devices):
    dofs, count = field.shape
    planes = devices // 4
    depth = -(-(dofs + 2) // 4)
    anywhere = pl.BlockSpec(memory_space=pl.ANY)
    wide = pltpu.VMEM((dofs, count), jnp.float32)
    blocks = pltpu.VMEM((devices, depth, LANES), jnp.float32)
    row = pltpu.VMEM((1, count), jnp.float32)
    parts = pltpu.VMEM((len(MATRIX_FACES), count // LANES * dofs // 6, 2 * LANES), jnp.bfloat16)
    dma = pltpu.SemaphoreType.DMA
    return pl.pallas_call(
        exchange_kernel,
        in_specs=[anywhere] * 9,
        out_specs=[pl.BlockSpec(memory_space=pltpu.VMEM), anywhere, anywhere],
        out_shape=[
            jax.ShapeDtypeStruct((1, count), jnp.float32),
            jax.ShapeDtypeStruct((devices, depth, LANES), jnp.float32),
            jax.ShapeDtypeStruct((2 * dofs, 3 * dofs), jnp.bfloat16),
        ],
        scratch_shapes=[
            wide, wide, pltpu.VMEM((2, dofs, count), jnp.float32), pltpu.VMEM((2, *face_nbrs.shape), jnp.int32),
            pltpu.VMEM(edge_signs.shape, jnp.int32),
            pltpu.VMEM(face_nbrs.shape, jnp.int32),
            row, row, pltpu.VMEM((1, count), jnp.int32),
            pltpu.VMEM(trace_map.shape, jnp.float32),
            pltpu.VMEM((8, count), jnp.float32),
            pltpu.VMEM((planes, LANES), jnp.int32),
            pltpu.VMEM((planes, LANES), jnp.int32),
            blocks, blocks,
            pltpu.VMEM((2, 1, count), jnp.float32), pltpu.VMEM((2, 1, count), jnp.float32), parts, parts,
            pltpu.VMEM((64 * -(-depth // 8), count), jnp.bfloat16), pltpu.VMEM((count, 2 * LANES), jnp.bfloat16),
            pltpu.VMEM((2, dofs, dofs), jnp.float32), pltpu.VMEM((2 * dofs, 3 * dofs), jnp.bfloat16),
            dma((CHUNKS + 8,)), dma((2, CHUNKS + 1)), dma((2, CHUNKS + 1)), dma, dma((planes,)), dma, dma, dma,
            dma((2,)), dma((2,)), dma,
        ],
        compiler_params=pltpu.CompilerParams(collective_id=0, has_side_effects=True, vmem_limit_bytes=VMEM_LIMIT),
        name="exchange",
    )(field, edge_signs, face_nbrs, mu, eps, owner, trace_map, stiffness, mass)


def apply_kernel(
    received_ref, both_ref, squares_ref, size_ref, migrated_ref, applied_ref, out_ref
):
    @pl.when(pl.program_id(0) == 0)
    def _():
        out_ref[...] = jnp.sqrt(size_ref[...] * (squares_ref[...] / migrated_ref.shape[0]) + 1e-06)

    lane = lax.broadcasted_iota(jnp.int32, (8, LANES), 1)
    dofs = migrated_ref.shape[0]
    groups = -(-received_ref.shape[1] // 8)
    tail = received_ref.shape[1] - 8 * (groups - 1)
    both = both_ref[...]
    for t in range(0, received_ref.shape[0] // 4, 2):
        cols = slice(t * LANES, (t + 2) * LANES)
        found = [[], []]
        for h in range(2):
            for i in range(groups):
                kept = 8 if i < groups - 1 else tail
                block = [received_ref[4 * (t + h) + q, 8 * i : 8 * i + kept, :] for q in range(4)]
                if kept < 8:
                    block = [jnp.concatenate([b, jnp.zeros((8 - kept, LANES), jnp.float32)], axis=0) for b in block]
                found[h].extend(piece[:kept] for piece in quarter_swap(block, lane))
        stacked = [jnp.concatenate(part, axis=0) for part in found]
        value = jnp.concatenate([part[:dofs] for part in stacked], axis=1)
        scale = jnp.concatenate([part[dofs : dofs + 2] for part in stacked], axis=1)
        migrated_ref[:, cols] = value
        product = stacked_product(both, value)
        applied_ref[:, cols] = scale[0:1] * product[:dofs] + scale[1:2] * product[dofs:]


def apply_received(received, both, squares, size):
    devices, depth, _ = received.shape
    dofs = both.shape[0] // 2
    per = 64
    block = per * 32
    return pl.pallas_call(
        apply_kernel,
        grid=(devices // per,),
        in_specs=[
            pl.BlockSpec((per, depth, LANES), lambda i: (i, 0, 0)),
            pl.BlockSpec(both.shape, lambda i: (0, 0)),
            pl.BlockSpec(squares.shape, lambda i: (0, 0)),
            pl.BlockSpec(squares.shape, lambda i: (0, 0)),
        ],
        out_specs=[pl.BlockSpec((dofs, block), lambda i: (0, i))] * 2 + [pl.BlockSpec(squares.shape, lambda i: (0, 0))],
        out_shape=[jax.ShapeDtypeStruct((dofs, devices * 32), jnp.float32)] * 2
        + [jax.ShapeDtypeStruct(squares.shape, jnp.float32)],
        compiler_params=pltpu.CompilerParams(vmem_limit_bytes=VMEM_LIMIT),
        cost_estimate=pl.CostEstimate(flops=10**9, bytes_accessed=8 * 10**6, transcendentals=0),
        name="apply",
    )(received, both, squares, size)


def body(field, edge_signs, face_nbrs, elem_size, mu_inv, permittivity, new_owner, trace_map, stiffness, mass):
    count = field.shape[1]
    devices = lax.axis_size(AXES)
    row = (1, count)
    squares, received, both = exchange(
        field, edge_signs, face_nbrs, mu_inv.reshape(row), permittivity.reshape(row), new_owner.reshape(row),
        trace_map, stiffness, mass, devices,
    )
    migrated, applied, indicators = apply_received(received, both, squares, elem_size.reshape(row))
    return indicators.reshape(count), migrated, applied


def solution(mesh):
    flat = P(AXES)
    wide = P(None, AXES)
    in_specs = (wide, wide, wide, flat, flat, flat, P(AXES, None), P(), P(), P())
    return jax.shard_map(body, mesh=mesh, in_specs=in_specs, out_specs=(flat, wide, wide), check_vma=False)
```

```python
import functools

import jax
import jax.numpy as jnp
from jax import lax
from jax.experimental import pallas as pl
from jax.experimental.pallas import tpu as pltpu
from jax.sharding import PartitionSpec as P

AXES = ("gx", "yz")
LANES = 128
VMEM_LIMIT = 60 << 20


def split3(value):
    high = value.astype(jnp.bfloat16)
    low = (value - high.astype(jnp.float32)).astype(jnp.bfloat16)
    return high, low


def stacked_left(matrix):
    high, low = split3(jnp.transpose(matrix))
    return jnp.concatenate([high, high, low], axis=1)


def stacked_product(left, right):
    high, low = split3(right)
    return jnp.dot(left, jnp.concatenate([high, low, high], axis=0), preferred_element_type=jnp.float32)


def lane_gather(table, index):
    return jnp.take_along_axis(table, index, axis=1)


def row8(row):
    return jnp.broadcast_to(row, (8, LANES))


def quarter_swap(parts, lane):
    upper = (lane & 64) != 0
    odd = (lane & 32) != 0
    a0, a1, a2, a3 = parts
    b0 = jnp.where(upper, pltpu.roll(a2, 64, 1), a0)
    b2 = jnp.where(upper, a2, pltpu.roll(a0, 64, 1))
    b1 = jnp.where(upper, pltpu.roll(a3, 64, 1), a1)
    b3 = jnp.where(upper, a3, pltpu.roll(a1, 64, 1))
    c0 = jnp.where(odd, pltpu.roll(b1, 32, 1), b0)
    c1 = jnp.where(odd, b1, pltpu.roll(b0, 96, 1))
    c2 = jnp.where(odd, pltpu.roll(b3, 32, 1), b2)
    c3 = jnp.where(odd, b3, pltpu.roll(b2, 96, 1))
    return c0, c1, c2, c3


MESH = pl.DeviceIdType.MESH
CHUNKS = 4
MATRIX_FACES = (0, 1, 3, 5)


def bit(k, n):
    return lax.rem(lax.div(k, 2**n), 2)


def offsets(k):
    return bit(k, 2) + 2 * bit(k, 3), bit(k, 4), bit(k, 0) + 2 * bit(k, 1)


def exchange_kernel(
    field_ref, signs_ref, nbrs_ref, mu_ref, eps_ref, owner_ref, map_ref, stiffness_ref, mass_ref,
    squares_ref, received_ref, both_ref,
    oriented, traces, halo_traces, halo_nbrs, signs, nbrs, mu, eps, owner, tmap, scale, high_ref, low_ref, payload, bundle,
    reply_out, reply_in, own_parts, halo_parts, columns, picks_ref, matrices, both,
    in_sem, halo_send, halo_recv, a_send, a_recv, f_send, f_recv, own_sem, reply_send, reply_recv, both_sem,
):
    gx = lax.axis_index("gx")
    yz = lax.axis_index("yz")
    gx_size = lax.axis_size("gx")
    yz_size = lax.axis_size("yz")
    devices = gx_size * yz_size
    me = gx * yz_size + yz
    z, c = lax.div(gx, 2), lax.rem(gx, 2)
    y, x = lax.div(yz, 4), lax.rem(yz, 4)
    plane = gx * 4 + y
    planes = devices // 4
    dofs, count = oriented.shape
    depth = payload.shape[1]
    block = count // CHUNKS

    def at(index):
        return (lax.div(index, yz_size), lax.rem(index, yz_size))

    def in_plane(p):
        return (lax.div(p, 4), lax.rem(p, 4) * 4 + x)

    def target(k):
        oz, oc, oy = offsets(k)
        return (lax.rem(z + oz, 4) * 2 + lax.rem(c + oc, 2)) * 4 + lax.rem(y + oy, 4)

    def source(k):
        oz, oc, oy = offsets(k)
        return (lax.rem(z + 4 - oz, 4) * 2 + lax.rem(c + 2 - oc, 2)) * 4 + lax.rem(y + 4 - oy, 4)

    following = lax.rem(me + 1, devices)
    preceding = lax.rem(me + devices - 1, devices)
    ahead, behind = at(following), at(preceding)
    up_index = jnp.where(c == 0, preceding, following)
    down_index = jnp.where(c == 0, following, preceding)
    up, down = at(up_index), at(down_index)
    sink = (c == 1) & (yz == 0)
    source_end = (c == 0) & (yz == 0)
    halo_count = jnp.where(sink, 2, jnp.where(source_end, 0, 1))
    landing_slot = jnp.where((c == 0) & (yz == yz_size - 1), 1, 0)
    reply_slot = jnp.where((c == 1) & (yz == yz_size - 1), 1, 0)

    loads = [
        pltpu.make_async_copy(signs_ref, signs, in_sem.at[0]),
        pltpu.make_async_copy(map_ref, tmap, in_sem.at[1]),
    ]
    fields = []
    for part in range(CHUNKS):
        cols = pl.ds(part * block, block)
        fields.append(pltpu.make_async_copy(field_ref.at[:, cols], oriented.at[:, cols], in_sem.at[2 + part]))
    later = [
        pltpu.make_async_copy(s, d, in_sem.at[2 + CHUNKS + i])
        for i, (s, d) in enumerate(
            (
                (owner_ref, owner), (mu_ref, mu), (eps_ref, eps), (nbrs_ref, nbrs),
                (stiffness_ref, matrices.at[0]), (mass_ref, matrices.at[1]),
            )
        )
    ]
    for copy in loads + fields + later:
        copy.start()

    barrier = pltpu.get_barrier_semaphore()

    def greet(k, carry):
        pl.semaphore_signal(barrier, inc=1, device_id=in_plane(target(k)), device_id_type=MESH)
        return carry

    lax.fori_loop(1, planes, greet, 0)
    for step in range(1, 4):
        pl.semaphore_signal(barrier, inc=1, device_id=(gx, y * 4 + lax.rem(x + step, 4)), device_id_type=MESH)
    pl.semaphore_signal(barrier, inc=1, device_id=ahead, device_id_type=MESH)
    pl.semaphore_signal(barrier, inc=1, device_id=behind, device_id_type=MESH)

    edges = signs.shape[0]
    rows = lax.broadcasted_iota(jnp.int32, (40, edges), 0)
    edge = lax.broadcasted_iota(jnp.int32, (40, edges), 1)
    picks = ((rows < 36) & (rows % 3 != 1) & (rows // 3 == edge)).astype(jnp.bfloat16)

    def halo_copy(part, lane_of, slot, peer):
        cols = pl.ds(part * block, block)
        if part == CHUNKS:
            src, dst = nbrs, halo_nbrs.at[slot]
        else:
            src, dst = traces.at[:, cols], halo_traces.at[slot, :, cols]
        return pltpu.make_async_remote_copy(
            src_ref=src, dst_ref=dst, send_sem=halo_send.at[lane_of, part], recv_sem=halo_recv.at[slot, part],
            device_id=peer, device_id_type=MESH,
        )

    def halo_start(part):
        @pl.when(jnp.logical_not(sink))
        def _():
            halo_copy(part, 0, landing_slot, down).start()

        @pl.when(source_end)
        def _():
            halo_copy(part, 1, 0, up).start()

    for copy in loads:
        copy.wait()
    map_parts = stacked_left(tmap[...])
    for part in range(CHUNKS):
        cols = slice(part * block, (part + 1) * block)
        fields[part].wait()
        shifted = (signs[:, cols] - 1).astype(jnp.float32).astype(jnp.bfloat16)
        factor = 1.0 + jnp.dot(picks, shifted, preferred_element_type=jnp.float32)
        oriented[0:40, cols] = oriented[0:40, cols] * factor
        traces[:, cols] = stacked_product(map_parts, oriented[:, cols])
        if part == 1:
            pl.semaphore_wait(barrier, planes - 1 + 3 + 2)
        if part >= 1:
            halo_start(part - 1)
    for copy in later:
        copy.wait()
    halo_start(CHUNKS)

    tiles = count // LANES
    bf = jnp.bfloat16
    sub = lax.broadcasted_iota(jnp.int32, (LANES, LANES), 0)
    lane_full = lax.broadcasted_iota(jnp.int32, (LANES, LANES), 1)
    upto = (sub <= lane_full).astype(jnp.float32).astype(bf)
    ones = jnp.ones((LANES, LANES), bf)
    before = jnp.zeros((LANES, LANES), jnp.float32)
    nt = (((1,), (1,)), ((), ()))
    table = jnp.zeros((3 * planes, LANES), jnp.float32)
    sub8 = lax.broadcasted_iota(jnp.int32, (8, LANES), 0)
    for tile in range(tiles):
        cols = slice(tile * LANES, (tile + 1) * LANES)
        scale[:, cols] = jnp.where(sub8 == 0, row8(mu[:, cols]), jnp.where(sub8 == 1, row8(eps[:, cols]), 0.0))
        own = owner[:, cols]
        onehot = sub == own
        hot = onehot.astype(jnp.float32)
        hot16 = hot.astype(bf)
        ordinal = before + jnp.dot(hot16, upto, preferred_element_type=jnp.float32) - 1.0
        rank = jnp.sum(jnp.where(onehot, ordinal, 0.0), axis=0, keepdims=True)
        before = before + jnp.dot(hot16, ones, preferred_element_type=jnp.float32)
        place = (own & 3) * 32 + rank.astype(jnp.int32)
        landing = (sub == place).astype(jnp.float32).astype(bf)
        group = lax.broadcasted_iota(jnp.int32, (planes, LANES), 0) == (own >> 2)
        groupf = group.astype(jnp.float32)
        lane_row = lax.broadcasted_iota(jnp.int32, (planes, LANES), 1).astype(jnp.float32)
        parts = jnp.concatenate([groupf, groupf * lane_row, groupf * float(tile)], axis=0).astype(bf)
        table = table + lax.dot_general(parts, landing, nt, preferred_element_type=jnp.float32)
    found = table[:planes]
    high_ref[...] = jnp.where(found > 0.5, table[2 * planes :], -1.0).astype(jnp.int32)
    low_ref[...] = table[planes : 2 * planes].astype(jnp.int32)
    halo_start(CHUNKS - 1)

    lane = lax.broadcasted_iota(jnp.int32, (8, LANES), 1)
    pair = 2 * LANES
    sub_pair = lax.broadcasted_iota(jnp.int32, (LANES, pair), 0)
    groups = -(-depth // 8)
    tail = depth - 8 * (groups - 1)
    height = 32 * groups
    main = 32 * (groups - 1)
    spot_row = lax.broadcasted_iota(jnp.int32, (32, dofs - main + 8), 0)
    item = lax.broadcasted_iota(jnp.int32, (32, dofs - main + 8), 1)
    inner = lax.rem(spot_row, 8)
    places = ((inner < tail) & (item == lax.div(spot_row, 8) * tail + inner)).astype(jnp.float32).astype(bf)
    for part in range(CHUNKS):
        cols = slice(part * block, (part + 1) * block)
        columns[0:main, cols], columns[height : height + main, cols] = split3(oriented[0:main, cols])
        rest_parts = split3(jnp.concatenate([oriented[main:, cols], scale[:, cols]], axis=0))
        for i, piece in enumerate(rest_parts):
            moved_rows = jnp.dot(places, piece, preferred_element_type=jnp.float32).astype(bf)
            columns[height * i + main : height * (i + 1), cols] = moved_rows

    def pack_pair(k):
        two = (target(k), target(k + 1))
        high = jnp.concatenate([high_ref[pl.ds(t, 1), :] for t in two], axis=1)
        low = jnp.concatenate([low_ref[pl.ds(t, 1), :] for t in two], axis=1)
        pick = (sub_pair == low).astype(jnp.float32).astype(bf)
        for tile in range(tiles):
            gate = jnp.broadcast_to((high == tile).astype(jnp.float32), (16, pair)).astype(bf)
            picks_ref[tile * LANES : (tile + 1) * LANES, :] = pick * jnp.concatenate([gate] * 8, axis=0)
        found = jnp.dot(columns[...], picks_ref[...], preferred_element_type=jnp.float32)
        value = found[:height] + found[height:]
        for h, t in enumerate(two):
            lanes = slice(h * LANES, (h + 1) * LANES)
            for i in range(groups):
                outs = quarter_swap([value[32 * i + 8 * q : 32 * i + 8 * q + 8, lanes] for q in range(4)], lane)
                kept = 8 if i < groups - 1 else tail
                for q in range(4):
                    payload[4 * t + q, 8 * i : 8 * i + kept, :] = outs[q][:kept]

    def send_group(k):
        t = target(k)
        pltpu.make_async_remote_copy(
            src_ref=payload.at[pl.ds(4 * t, 4)], dst_ref=bundle.at[pl.ds(4 * plane, 4)], send_sem=a_send,
            recv_sem=a_recv.at[plane], device_id=in_plane(t), device_id_type=MESH,
        ).start()

    def forward(origin, s):
        for step in range(1, 4):
            xd = lax.rem(x + step, 4)
            pltpu.make_async_remote_copy(
                src_ref=origin.at[4 * s + xd], dst_ref=received_ref.at[4 * s + x], send_sem=f_send, recv_sem=f_recv,
                device_id=(gx, y * 4 + xd), device_id_type=MESH,
            ).start()
        pltpu.make_async_copy(origin.at[4 * s + x], received_ref.at[4 * s + x], own_sem).start()

    def forward_step(k):
        s = source(k)
        pltpu.make_async_remote_copy(
            src_ref=payload.at[pl.ds(4 * s, 4)], dst_ref=bundle.at[pl.ds(4 * s, 4)], send_sem=a_send,
            recv_sem=a_recv.at[s], device_id=ahead, device_id_type=MESH,
        ).wait_recv()
        forward(bundle, s)

    lag = 9

    def pack_step(m, carry):
        pack_pair(2 * m)

        @pl.when(m == 1)
        def _():
            forward(payload, plane)

        @pl.when(m > 1)
        def _():
            send_group(2 * m - 2)

        @pl.when(m > 0)
        def _():
            send_group(2 * m - 1)

        @pl.when(m >= lag)
        def _():
            forward_step(m - lag + 1)

        return carry

    lax.fori_loop(0, planes // 2, pack_step, 0)
    send_group(planes - 2)
    send_group(planes - 1)
    done = planes // 2 - lag + 1

    width = dofs // 6
    vecs = width // 8

    def split_table(table, out):
        for o, odd in enumerate(MATRIX_FACES):
            rows_o = slice(odd * width, (odd + 1) * width)
            for tile in range(0, tiles, 2):
                stacked = jnp.concatenate(
                    [table[rows_o, (tile + i) * LANES : (tile + i + 1) * LANES] for i in range(2)], axis=0
                )
                high, low = split3(stacked)
                out[o, tile * width : (tile + 2) * width, 0:LANES] = high
                out[o, tile * width : (tile + 2) * width, LANES:] = low

    def jump_tile(step, faces, face_nbrs, table, parts, base, alone):
        cols = pl.ds(pl.multiple_of(step * pair, pair), pair)
        total = jnp.zeros((8, pair), jnp.float32)
        for face in range(6):
            other = face ^ 1
            nbr = jnp.broadcast_to(face_nbrs[face : face + 1, cols], (8, pair))
            spot = nbr - base
            high = spot >> 7
            low = spot & (LANES - 1)
            if other in MATRIX_FACES:
                pick = (sub_pair == low[0:1]).astype(jnp.float32).astype(jnp.bfloat16)
                found = jnp.dot(
                    parts[MATRIX_FACES.index(other)], jnp.concatenate([pick, pick], axis=0), preferred_element_type=jnp.float32
                )
                got = [jnp.zeros((8, pair), jnp.float32) for _ in range(vecs)]
                for tile in range(tiles):
                    hit = high == tile
                    for v in range(vecs):
                        r = tile * width + 8 * v
                        got[v] = jnp.where(hit, found[r : r + 8], got[v])
            else:
                halves = []
                for h in range(2):
                    lanes = slice(h * LANES, (h + 1) * LANES)
                    half = [jnp.zeros((8, LANES), jnp.float32) for _ in range(vecs)]
                    for tile in range(tiles):
                        hit = high[:, lanes] == tile
                        for v in range(vecs):
                            r = other * width + 8 * v
                            piece = table[r : r + 8, tile * LANES : (tile + 1) * LANES]
                            half[v] = jnp.where(hit, lane_gather(piece, low[:, lanes]), half[v])
                    halves.append(half)
                got = [jnp.concatenate([halves[0][v], halves[1][v]], axis=1) for v in range(vecs)]
            here = (spot >= 0) & (spot < count)
            if alone:
                here = here | (nbr < 0)
            for v in range(vecs):
                r = face * width + 8 * v
                jump = faces[r : r + 8, cols] - got[v]
                total = total + jnp.where(here, jump * jump, 0.0)
        return cols, jnp.sum(total, axis=0, keepdims=True)

    own_base = me * count

    for i in range(2):
        both[dofs * i : dofs * (i + 1)] = stacked_left(matrices[i])
    hand_over = pltpu.make_async_copy(both, both_ref, both_sem)
    split_table(traces, own_parts)

    hand_over.start()

    def own_step(step, carry):
        forward_step(done + step)
        cols, row = jump_tile(step, traces, nbrs, traces, own_parts, own_base, True)
        squares_ref[:, cols] = row
        return carry

    lax.fori_loop(0, tiles // 2, own_step, 0)
    rest = done + tiles // 2

    def halo_step(i, carry):
        for part in range(CHUNKS + 1):
            halo_copy(part, 0, i, up).wait_recv()
        base = jnp.where(i == 0, up_index, down_index) * count
        split_table(halo_traces.at[i], halo_parts)

        def across(step, inner):
            first = rest + jnp.where(sink, i * (tiles // 2) + step, 2 * step)
            second = rest + 2 * step + 1

            @pl.when(first < planes)
            def _():
                forward_step(first)

            @pl.when(jnp.logical_not(sink) & (second < planes))
            def _():
                forward_step(second)

            cols, row = jump_tile(step, traces, nbrs, halo_traces.at[i], halo_parts, base, False)
            squares_ref[:, cols] = squares_ref[:, cols] + row
            cols, row = jump_tile(step, halo_traces.at[i], halo_nbrs.at[i], traces, own_parts, own_base, False)
            reply_out[i, :, cols] = row
            return inner

        lax.fori_loop(0, tiles // 2, across, 0)
        return carry

    lax.fori_loop(0, halo_count, halo_step, 0)

    @pl.when(source_end)
    def _():
        def remaining(k, carry):
            forward_step(k)
            return carry

        lax.fori_loop(rest, planes, remaining, 0)

    def reply(slot, landing, peer):
        return pltpu.make_async_remote_copy(
            src_ref=reply_out.at[slot], dst_ref=reply_in.at[landing], send_sem=reply_send.at[slot],
            recv_sem=reply_recv.at[landing], device_id=peer, device_id_type=MESH,
        )

    @pl.when(jnp.logical_not(source_end))
    def _():
        reply(0, reply_slot, up).start()

    @pl.when(sink)
    def _():
        reply(1, 0, down).start()

    @pl.when(jnp.logical_not(sink))
    def _():
        reply(0, 0, up).wait_recv()
        squares_ref[...] = squares_ref[...] + reply_in[0]

    @pl.when(source_end)
    def _():
        reply(0, 1, up).wait_recv()
        squares_ref[...] = squares_ref[...] + reply_in[1]

    hand_over.wait()
    @pl.when(jnp.logical_not(source_end))
    def _():
        reply(0, reply_slot, up).wait_send()

    @pl.when(sink)
    def _():
        reply(1, 0, down).wait_send()

    for part in range(CHUNKS + 1):

        @pl.when(jnp.logical_not(sink))
        def _():
            halo_copy(part, 0, landing_slot, down).wait_send()

        @pl.when(source_end)
        def _():
            halo_copy(part, 1, 0, up).wait_send()

    sent = 4 * (planes - 1)
    pltpu.make_async_remote_copy(
        src_ref=payload.at[pl.ds(0, sent)], dst_ref=bundle.at[pl.ds(0, sent)], send_sem=a_send, recv_sem=a_recv.at[0],
        device_id=ahead, device_id_type=MESH,
    ).wait_send()
    moved = 3 * planes
    along = pltpu.make_async_remote_copy(
        src_ref=bundle.at[pl.ds(0, moved)], dst_ref=received_ref.at[pl.ds(0, moved)], send_sem=f_send, recv_sem=f_recv,
        device_id=ahead, device_id_type=MESH,
    )
    along.wait_send()
    along.wait_recv()
    pltpu.make_async_copy(bundle.at[pl.ds(0, planes)], received_ref.at[pl.ds(0, planes)], own_sem).wait()


def exchange(field, edge_signs, face_nbrs, mu, eps, owner, trace_map, stiffness, mass, devices):
    dofs, count = field.shape
    planes = devices // 4
    depth = -(-(dofs + 2) // 4)
    anywhere = pl.BlockSpec(memory_space=pl.ANY)
    wide = pltpu.VMEM((dofs, count), jnp.float32)
    blocks = pltpu.VMEM((devices, depth, LANES), jnp.float32)
    row = pltpu.VMEM((1, count), jnp.float32)
    parts = pltpu.VMEM((len(MATRIX_FACES), count // LANES * dofs // 6, 2 * LANES), jnp.bfloat16)
    dma = pltpu.SemaphoreType.DMA
    return pl.pallas_call(
        exchange_kernel,
        in_specs=[anywhere] * 9,
        out_specs=[pl.BlockSpec(memory_space=pltpu.VMEM), anywhere, anywhere],
        out_shape=[
            jax.ShapeDtypeStruct((1, count), jnp.float32),
            jax.ShapeDtypeStruct((devices, depth, LANES), jnp.float32),
            jax.ShapeDtypeStruct((2 * dofs, 3 * dofs), jnp.bfloat16),
        ],
        scratch_shapes=[
            wide, wide, pltpu.VMEM((2, dofs, count), jnp.float32), pltpu.VMEM((2, *face_nbrs.shape), jnp.int32),
            pltpu.VMEM(edge_signs.shape, jnp.int32),
            pltpu.VMEM(face_nbrs.shape, jnp.int32),
            row, row, pltpu.VMEM((1, count), jnp.int32),
            pltpu.VMEM(trace_map.shape, jnp.float32),
            pltpu.VMEM((8, count), jnp.float32),
            pltpu.VMEM((planes, LANES), jnp.int32),
            pltpu.VMEM((planes, LANES), jnp.int32),
            blocks, blocks,
            pltpu.VMEM((2, 1, count), jnp.float32), pltpu.VMEM((2, 1, count), jnp.float32), parts, parts,
            pltpu.VMEM((64 * -(-depth // 8), count), jnp.bfloat16), pltpu.VMEM((count, 2 * LANES), jnp.bfloat16),
            pltpu.VMEM((2, dofs, dofs), jnp.float32), pltpu.VMEM((2 * dofs, 3 * dofs), jnp.bfloat16),
            dma((CHUNKS + 8,)), dma((2, CHUNKS + 1)), dma((2, CHUNKS + 1)), dma, dma((planes,)), dma, dma, dma,
            dma((2,)), dma((2,)), dma,
        ],
        compiler_params=pltpu.CompilerParams(collective_id=0, has_side_effects=True, vmem_limit_bytes=VMEM_LIMIT),
        name="exchange",
    )(field, edge_signs, face_nbrs, mu, eps, owner, trace_map, stiffness, mass)


def apply_kernel(
    received_ref, both_ref, squares_ref, size_ref, migrated_ref, applied_ref, out_ref
):
    @pl.when(pl.program_id(0) == 0)
    def _():
        out_ref[...] = jnp.sqrt(size_ref[...] * (squares_ref[...] / migrated_ref.shape[0]) + 1e-06)

    lane = lax.broadcasted_iota(jnp.int32, (8, LANES), 1)
    dofs = migrated_ref.shape[0]
    groups = -(-received_ref.shape[1] // 8)
    tail = received_ref.shape[1] - 8 * (groups - 1)
    both = both_ref[...]
    for t in range(0, received_ref.shape[0] // 4, 2):
        cols = slice(t * LANES, (t + 2) * LANES)
        found = [[], []]
        for h in range(2):
            for i in range(groups):
                kept = 8 if i < groups - 1 else tail
                block = [received_ref[4 * (t + h) + q, 8 * i : 8 * i + kept, :] for q in range(4)]
                if kept < 8:
                    block = [jnp.concatenate([b, jnp.zeros((8 - kept, LANES), jnp.float32)], axis=0) for b in block]
                found[h].extend(piece[:kept] for piece in quarter_swap(block, lane))
        stacked = [jnp.concatenate(part, axis=0) for part in found]
        value = jnp.concatenate([part[:dofs] for part in stacked], axis=1)
        scale = jnp.concatenate([part[dofs : dofs + 2] for part in stacked], axis=1)
        migrated_ref[:, cols] = value
        product = stacked_product(both, value)
        applied_ref[:, cols] = scale[0:1] * product[:dofs] + scale[1:2] * product[dofs:]


def apply_received(received, both, squares, size):
    devices, depth, _ = received.shape
    dofs = both.shape[0] // 2
    per = 64
    block = per * 32
    return pl.pallas_call(
        apply_kernel,
        grid=(devices // per,),
        in_specs=[
            pl.BlockSpec((per, depth, LANES), lambda i: (i, 0, 0)),
            pl.BlockSpec(both.shape, lambda i: (0, 0)),
            pl.BlockSpec(squares.shape, lambda i: (0, 0)),
            pl.BlockSpec(squares.shape, lambda i: (0, 0)),
        ],
        out_specs=[pl.BlockSpec((dofs, block), lambda i: (0, i))] * 2 + [pl.BlockSpec(squares.shape, lambda i: (0, 0))],
        out_shape=[jax.ShapeDtypeStruct((dofs, devices * 32), jnp.float32)] * 2
        + [jax.ShapeDtypeStruct(squares.shape, jnp.float32)],
        compiler_params=pltpu.CompilerParams(vmem_limit_bytes=VMEM_LIMIT),
        cost_estimate=pl.CostEstimate(flops=10**9, bytes_accessed=8 * 10**6, transcendentals=0),
        name="apply",
    )(received, both, squares, size)


def body(field, edge_signs, face_nbrs, elem_size, mu_inv, permittivity, new_owner, trace_map, stiffness, mass):
    count = field.shape[1]
    devices = lax.axis_size(AXES)
    row = (1, count)
    squares, received, both = exchange(
        field, edge_signs, face_nbrs, mu_inv.reshape(row), permittivity.reshape(row), new_owner.reshape(row),
        trace_map, stiffness, mass, devices,
    )
    migrated, applied, indicators = apply_received(received, both, squares, elem_size.reshape(row))
    return indicators.reshape(count), migrated, applied


def solution(mesh):
    flat = P(AXES)
    wide = P(None, AXES)
    in_specs = (wide, wide, wide, flat, flat, flat, P(AXES, None), P(), P(), P())
    return jax.shard_map(body, mesh=mesh, in_specs=in_specs, out_specs=(flat, wide, wide), check_vma=False)
```
